32 devices in a mesh: img: 2 (over y), cls: 4 (over z), emb: 4 (over x, core).
Axes of the slice: x: 2, y: 2, z: 4, core: 2. Of those that a mesh axis runs over, the one named last changes fastest.
Arguments:
- regions: bfloat16 [2048, 1024], P('img', 'emb'), may hold values from -8 to 8
- table: bfloat16 [21504, 1024], P('cls', 'emb'), may hold values from -1 to 1
- shift: float32 [2048], P('img'), may hold values from -0.5 to 0.1
- scale: float32 [2048], P('img'), may hold values from 2 to 20
- labels: int32 [2048], P('img'), may hold values from -1 to 21503, as said below
- valid: int32 [4, 21504], P('img', 'cls'), may hold values 0 or 1
Outputs:
- loss: float32 [], replicated
- region_grad: bfloat16 [2048, 1024], P('img', 'emb')
- table_grad: bfloat16 [21504, 1024], P('cls', 'emb')
The draws below stay inside these ranges and needn't reach their ends.
Inputs may be any that keep to these rules, and one draw needn't show every extreme that they name: `labels`: -1 marks background; the first region of every image is foreground.
All inputs are finite; a program needn't handle non-finite values. No bound on the sum of `valid` on one device may be relied on, other than what follows from the above.
Results may differ from the reference program's by a relative error of at most 0.0034.
Values may be sent and summed in bfloat16 or wider, within the bound.
A program may use at most 64 MiB of HBM per device.

```python
import math
import jax
import jax.numpy as jnp
from jax import lax

D = 1024
CLASSES = 21504
REG_IMG = 512
IMG_DEV = 2
IMAGES = 4
REGIONS = 2048


cluster_count = 64


def make_labels(key):
    key_fg = jax.random.fold_in(key, 11)
    key_cls = jax.random.fold_in(key, 23)
    position = jnp.arange(REGIONS, dtype=jnp.int32)
    image = position // REG_IMG
    within = position % REG_IMG
    threshold = 150 + 350 * image // max(IMAGES - 1, 1)
    roll = jax.random.randint(key_fg, (REGIONS,), 0, 1000, dtype=jnp.int32)
    chosen = jax.random.randint(key_cls, (REGIONS,), 0, CLASSES, dtype=jnp.int32)
    foreground = (roll < threshold) | (within == 0)
    return jnp.where(foreground, chosen, -1).astype(jnp.int32)


def make_table(key):
    key_dir = jax.random.fold_in(key, 41)
    key_own = jax.random.fold_in(key, 43)
    directions = jax.random.normal(key_dir, (cluster_count, D), jnp.float32)
    directions = directions * lax_rsqrt(jnp.sum(directions * directions, axis=1, keepdims=True))
    own = jax.random.normal(key_own, (CLASSES, D), jnp.float32)
    mixing = 0.6
    own = own * lax_rsqrt(jnp.sum(own * own, axis=1, keepdims=True))
    cluster = jnp.arange(CLASSES, dtype=jnp.int32) % cluster_count
    shared = directions[cluster]
    mixed = mixing * shared + (1.0 - mixing * mixing) ** 0.5 * own
    mixed = mixed * lax_rsqrt(jnp.sum(mixed * mixed, axis=1, keepdims=True))
    return (mixed, directions)


def lax_rsqrt(value):
    return 1.0 / jnp.sqrt(value)


def draw_labels(key, part):
    return make_labels(key)


def draw_table(key, part):
    mixed, directions = make_table(key)
    return jnp.clip(mixed, -1.0, 1.0).astype(jnp.bfloat16)


def draw_regions(key, part):
    labels = make_labels(key)
    mixed, directions = make_table(key)
    foreground = labels >= 0
    safe_labels = jnp.maximum(labels, 0)
    background = jax.random.randint(jax.random.fold_in(key, 31), (REGIONS,), 0, cluster_count, dtype=jnp.int32)
    aim = jnp.where(foreground[:, None], mixed[safe_labels], directions[background])
    key_str = jax.random.fold_in(key, 53)
    key_noise = jax.random.fold_in(key, 59)
    key_mag = jax.random.fold_in(key, 61)
    strength = jax.random.uniform(key_str, (REGIONS, 1), jnp.float32, 0.5, 1.2)
    noise = jax.random.normal(key_noise, (REGIONS, D), jnp.float32)
    magnitude = jnp.exp(jax.random.uniform(key_mag, (REGIONS, 1), jnp.float32, -1.386, 0.0))
    region = magnitude * (strength * aim * D ** 0.5 + noise)
    return jnp.clip(region, -8.0, 8.0).astype(jnp.bfloat16)


def place_ends(drawn, own_key, least, largest):
    extent = drawn.shape
    index_at = [jax.random.randint(jax.random.fold_in(own_key, axis), (), 0, extent[axis]) for axis in range(len(extent))]
    drawn = drawn.at[tuple(index_at)].set(least)
    longest = extent.index(max(extent))
    index_at[longest] = (index_at[longest] + 1) % extent[longest]
    return drawn.at[tuple(index_at)].set(largest)


def steps_of(stream_key, shape, cuts, least, top_value):
    def one(dim, parts):
        heights = jax.random.uniform(jax.random.fold_in(jax.random.fold_in(stream_key, 6), dim), (parts,), jnp.float32, least / len(cuts), top_value / len(cuts))
        return jnp.repeat(jnp.exp(heights), shape[dim] // parts).reshape((-1,) + (1,) * (len(shape) - dim - 1))

    factor_of = one(*cuts[0])
    for cut in cuts[1:]:
        factor_of = factor_of * one(*cut)
    return factor_of


def setup_inputs(seed: int = 0) -> dict:
    key_list = jax.random.split(jax.random.key(seed), 7)
    regions = draw_regions(jax.random.fold_in(key_list[6], 71), 0)
    table = draw_table(jax.random.fold_in(key_list[6], 71), 0)
    shift = jnp.clip(-0.5 + 0.6 * jax.random.uniform(key_list[2], (REGIONS,), jnp.float32) ** steps_of(key_list[2], (REGIONS,), ((0, 2),), -0.2, 0.2), -0.5, 0.1)
    scale = jnp.clip(jnp.exp(math.log(20.0) - 2.3025851 * jax.random.uniform(key_list[3], (REGIONS,), jnp.float32) ** steps_of(key_list[3], (REGIONS,), ((0, 2),), -0.2, 0.2)), 2.0, 20.0)
    labels = draw_labels(jax.random.fold_in(key_list[6], 71), 0)
    valid = place_ends((jax.random.randint(key_list[5], (IMAGES, CLASSES), 0, 4) < 3).astype(jnp.int32), jax.random.fold_in(key_list[5], 1), 0, 1)
    return dict(regions=regions, table=table, shift=shift, scale=scale, labels=labels, valid=valid)


def focal(logit, target):
    prob = jax.nn.sigmoid(logit)
    return -0.25 * target * (1.0 - prob) ** 2 * jax.nn.log_sigmoid(logit) - 0.75 * (1.0 - target) * prob ** 2 * jax.nn.log_sigmoid(-logit)

def reference(regions, table, shift, scale, labels, valid):
    rows = IMG_DEV * REG_IMG
    blocks = REGIONS // rows
    count = jnp.sum((labels >= 0).astype(jnp.float32))
    factor = REGIONS / count
    class_ids = jnp.arange(CLASSES, dtype=jnp.int32)

    def step(carry, index):
        total, table_acc = carry
        start = (index * rows).astype(jnp.int32)
        block = lax.dynamic_slice_in_dim(regions, start, rows, 0).astype(jnp.float32)
        inv = lax.rsqrt(lax.optimization_barrier(jnp.sum(block * block, axis=1)) + 1e-06)
        unit = block * inv[:, None]
        unit_b = unit.astype(jnp.bfloat16)
        cosine = jnp.dot(unit_b, table.T, preferred_element_type=jnp.float32)
        shift_b = lax.dynamic_slice_in_dim(shift, start, rows, 0)
        scale_b = lax.dynamic_slice_in_dim(scale, start, rows, 0)
        label_b = lax.dynamic_slice_in_dim(labels, start, rows, 0)
        valid_b = lax.dynamic_slice_in_dim(valid, (index * IMG_DEV).astype(jnp.int32), IMG_DEV, 0).astype(jnp.float32)
        image_ids = jnp.arange(rows, dtype=jnp.int32) // REG_IMG
        onehot = (image_ids[:, None] == jnp.arange(IMG_DEV, dtype=jnp.int32)[None, :]).astype(jnp.float32)
        mask = jnp.dot(onehot, valid_b, preferred_element_type=jnp.float32)
        logit = (cosine + shift_b[:, None]) * scale_b[:, None]
        target = (label_b[:, None] == class_ids[None, :]).astype(jnp.float32)
        term, pullback = jax.vjp(lambda value: focal(value, target), logit)
        dlogit = pullback(jnp.ones_like(term))[0]
        total = total + jnp.sum(term * mask)
        dscore = (dlogit * mask * scale_b[:, None] * factor).astype(jnp.bfloat16)
        dunit = jnp.dot(dscore, table, preferred_element_type=jnp.float32)
        radial = lax.optimization_barrier(jnp.sum(unit * dunit, axis=1))
        grad_b = (inv[:, None] * (dunit - unit * radial[:, None])).astype(jnp.bfloat16)
        table_acc = table_acc + jnp.dot(dscore.T, unit_b, preferred_element_type=jnp.float32)
        return ((total, table_acc), grad_b)
    init = (jnp.zeros((), jnp.float32), jnp.zeros((CLASSES, D), jnp.float32))
    (total, table_acc), grads = lax.scan(step, init, jnp.arange(blocks, dtype=jnp.int32))
    loss = total / count / CLASSES
    return (loss, grads.reshape(REGIONS, D), table_acc.astype(jnp.bfloat16))
```

```python
import functools

import jax
import jax.numpy as jnp
from jax import lax
from jax.experimental import pallas as pl
from jax.experimental.pallas import tpu as pltpu
from jax.sharding import PartitionSpec as P

MESH = pl.DeviceIdType.MESH
F32 = jnp.float32
BF16 = jnp.bfloat16


def kernel(cfg, regions, table, packed, valid, loss_out, rg_out, tg_out,
           RG, UN, TB, DS, SC, VB, SP, KP, PR, XS, XR, YS, YR, ZS, ZR,
           TS, LA, LE, LI, LC, RD, RO,
           loc, g_send, g_recv, t_send, t_recv, s_send, s_recv,
           p_send, p_recv, x_send, x_recv, y_send, y_recv, z_send, z_recv,
           o_send, o_recv, f_send, f_recv, l_send, l_recv, r_send, r_recv,
           w_send, w_recv):
    n_i, n_c, n_e, rows, width, blk, pad, classes, imgs = cfg
    i, c, e = lax.axis_index("img"), lax.axis_index("cls"), lax.axis_index("emb")
    k = lax.rem(e, 2)
    x = e // 2
    oi = 1 - i
    part = 2 * x + 1 - k
    xn = 2 * (1 - x) + k
    xp = 2 * (1 - x) + 1 - k
    j = i * n_e + e
    ch = rows // n_c
    n_t = 2 * n_c
    full = n_e * width

    def dev(ii, cc, ee):
        return (ii, cc, ee)

    def rcopy(src, dst, ss, rs, d):
        return pltpu.make_async_remote_copy(
            src_ref=src, dst_ref=dst, send_sem=ss, recv_sem=rs,
            device_id=d, device_id_type=MESH)

    def cols(q):
        return pl.ds(pl.multiple_of(q * width, width), width)

    def rblk(q):
        return pl.ds(pl.multiple_of(q * blk, 16), blk)

    barrier = pltpu.get_barrier_semaphore()
    for ee in (part, xn, xp):
        pl.semaphore_signal(barrier, inc=1, device_id=dev(i, c, ee), device_id_type=MESH)
    pl.semaphore_signal(barrier, inc=1, device_id=dev(oi, c, e), device_id_type=MESH)
    for s in range(1, n_c):
        pl.semaphore_signal(barrier, inc=1, device_id=dev(i, lax.rem(c + s, n_c), e), device_id_type=MESH)
    pl.semaphore_wait(barrier, 3 + 1 + n_c - 1)

    d_part, d_xn, d_xp, d_y = dev(i, c, part), dev(i, c, xn), dev(i, c, xp), dev(oi, c, e)

    own_x = rcopy(regions, RG.at[i, :, cols(e)], g_send.at[0], g_recv.at[0], d_xn)
    own_y = rcopy(regions, RG.at[i, :, cols(e)], g_send.at[1], g_recv.at[1], d_y)
    own_p = rcopy(regions, RG.at[i, :, cols(e)], g_send.at[2], g_recv.at[3], d_part)
    own_x.start()
    own_y.start()
    own_p.start()
    sc_y = rcopy(packed, SC.at[i], s_send.at[0], s_recv.at[0], d_y)
    sc_y.start()
    jy = oi * n_e + e
    v_y = rcopy(valid.at[jy], VB.at[i], s_send.at[1], s_recv.at[1], d_y)
    v_y.start()
    tcopies = []
    for n, ee in enumerate((xn, xp, part)):
        t = rcopy(table.at[rblk(i * n_e + ee), :], TB.at[pl.ds(0, blk), cols(e)],
                  t_send.at[n], t_recv.at[n], dev(i, c, ee))
        t.start()
        tcopies.append(t)
    locs = [
        pltpu.make_async_copy(regions, RG.at[i, :, cols(e)], loc.at[0]),
        pltpu.make_async_copy(table.at[rblk(j), :], TB.at[pl.ds(0, blk), cols(e)], loc.at[1]),
        pltpu.make_async_copy(packed, SC.at[i], loc.at[2]),
        pltpu.make_async_copy(valid.at[j], VB.at[i], loc.at[3]),
    ]
    for q in locs:
        q.start()
    TB[pl.ds(blk, pad - blk), :] = jnp.zeros((pad - blk, full), BF16)
    LA[...] = jnp.zeros_like(LA)

    own_x.wait_recv()
    rel_p = rcopy(RG.at[i, :, cols(xn)], RG.at[i, :, cols(xn)], g_send.at[3], g_recv.at[4], d_part)
    rel_y = rcopy(RG.at[i, :, cols(xn)], RG.at[i, :, cols(xn)], g_send.at[4], g_recv.at[2], d_y)
    rel_y.start()
    rel_p.start()
    own_y.wait_recv()
    fy1 = rcopy(RG.at[oi, :, cols(e)], RG.at[oi, :, cols(e)], g_send.at[5], g_recv.at[5], d_part)
    fy1.start()
    rel_y.wait_recv()
    fy2 = rcopy(RG.at[oi, :, cols(xn)], RG.at[oi, :, cols(xn)], g_send.at[6], g_recv.at[6], d_part)
    fy2.start()
    for q in locs:
        q.wait()
    sc_y.wait_recv()
    v_y.wait_recv()
    own_p.wait_recv()
    rel_p.wait_recv()
    fy1.wait_recv()
    fy2.wait_recv()
    for t in tcopies:
        t.wait_recv()

    labels0 = SC[0, 2:3, :]
    labels1 = SC[1, 2:3, :]
    count = jnp.sum((labels0 >= 0).astype(F32) + (labels1 >= 0).astype(F32), axis=1, keepdims=True)
    factor = (rows * n_i) / count

    base = (c * (n_i * n_e) + j) * blk
    class_ids = (base + lax.broadcasted_iota(jnp.int32, (1, pad), 1)).astype(F32)
    per_img = rows // imgs

    def place(t):
        return lax.rem(t // n_c + 1 + i, 2), lax.rem(t, n_c)

    def pcopy(t):
        return rcopy(SP.at[t], PR.at[t], p_send.at[t], p_recv.at[t], d_part)

    def xcopy(t):
        return rcopy(XS.at[t], XR.at[t], x_send.at[t], x_recv.at[t], d_xn)

    def ycopy(t):
        return rcopy(YS.at[t], YR.at[t], y_send.at[t], y_recv.at[t], d_y)

    def zcopy(m):
        return rcopy(ZS.at[m], ZR.at[c], z_send.at[m], z_recv.at[c], dev(i, m, e))

    def compute(t):
        im, m = place(t)
        r0 = pl.multiple_of(m * ch, ch)
        block = RG[im, pl.ds(r0, ch), :].astype(F32)
        inv = lax.rsqrt(jnp.sum(block * block, axis=1, keepdims=True) + 1e-06)
        unit_b = (block * inv).astype(BF16)
        u0 = pl.multiple_of(im * rows + m * ch, ch)
        UN[pl.ds(u0, ch), :] = unit_b
        cosine = lax.dot_general(unit_b, TB[...], (((1,), (1,)), ((), ())),
                                 preferred_element_type=F32)
        cc = SC[im, :, pl.ds(r0, ch)].T
        shift, scale, label = cc[:, 0:1], cc[:, 1:2], cc[:, 2:3]
        mask = VB[im, (m * ch) // per_img][0:1, :]
        z = (cosine + shift) * scale
        hit = label == class_ids
        s = jnp.where(hit, -z, z)
        ex = jnp.exp(-jnp.abs(s))
        den = 1.0 + ex
        r = 1.0 / den
        er = ex * r
        pos = s >= 0
        q = jnp.where(pos, r, er)
        nq = jnp.where(pos, er, r)
        lg = jnp.where(ex < 0.01, ex * (1.0 - ex * (0.5 - ex * (1.0 / 3.0))), jnp.log(den))
        soft = jnp.maximum(s, 0.0) + lg
        wq = jnp.where(hit, 0.25, 0.75) * (q * q) * mask
        term = wq * soft
        LA[...] += jnp.sum(term.reshape(ch // 8, 8, pad), axis=0)
        g = wq * (q + 2.0 * nq * soft)
        g = jnp.where(hit, -g, g) * (scale * factor)
        ds = g.astype(BF16)
        DS[:, pl.ds(u0, ch)] = ds.T
        for xi in range(2):
            SP[t, xi] = jnp.dot(ds, TB[:, cols(2 * xi + 1 - k)], preferred_element_type=F32)
            KP[t, xi] = jnp.dot(ds, TB[:, cols(2 * xi + k)], preferred_element_type=F32)
        pcopy(t).start()

    def stage2(t):
        pcopy(t).wait_recv()
        XS[t] = (KP[t, 1 - x] + PR[t, 1 - x]).astype(BF16)
        xcopy(t).start()
        KP[t, x] = KP[t, x] + PR[t, x]

    def stage3(t):
        xcopy(t).wait_recv()
        val = KP[t, x] + XR[t].astype(F32)

        @pl.when(t < n_c)
        def _():
            YS[t] = val.astype(BF16)
            ycopy(t).start()

        @pl.when(t >= n_c)
        def _():
            m = t - n_c
            ycopy(m).wait_recv()
            tot = val + YR[m].astype(F32)

            @pl.when(m == c)
            def _():
                ZR[m] = tot

            @pl.when(m != c)
            def _():
                ZS[m] = tot
                zcopy(m).start()

    @pl.loop(0, n_t + 2)
    def _(t):
        @pl.when(t < n_t)
        def _():
            compute(t)

        @pl.when((t >= 1) & (t < n_t + 1))
        def _():
            stage2(t - 1)

        @pl.when(t >= 2)
        def _():
            stage3(t - 2)

    tile = LA[:, 0:128]
    for b in range(1, pad // 128):
        tile = tile + LA[:, b * 128:(b + 1) * 128]
    LE[e] = tile
    lcs = []
    for n, ee in enumerate((part, xn, xp)):
        lc = rcopy(LE.at[e], LE.at[e], l_send.at[n], l_recv.at[e], dev(i, c, ee))
        lc.start()
        lcs.append(lc)

    def ocopy(n, q):
        return rcopy(TS.at[n], tg_out.at[rblk(j), :], o_send.at[n], o_recv.at[n], dev(i, c, q))

    targets = (xn, xp, part, e)
    dst_of = []

    def tg_of(n, q):
        TS[n] = jnp.dot(DS[0:blk, :], UN[:, cols(q)], preferred_element_type=F32).astype(BF16)

    @pl.loop(0, 4)
    def _(n):
        xx = jnp.where(n < 2, 1 - x, x)
        kk = jnp.where((n == 0) | (n == 3), k, 1 - k)
        q = 2 * xx + kk
        tg_of(n, q)

        @pl.when(n < 3)
        def _():
            ocopy(n, q).start()

    own_o = pltpu.make_async_copy(TS.at[3], tg_out.at[rblk(j), :], loc.at[4])
    own_o.start()

    def fcopy(n, q):
        src = TS.at[3] if n == 3 else tg_out.at[rblk(i * n_e + q), :]
        return rcopy(src, tg_out.at[rblk(i * n_e + q), :], f_send.at[n], f_recv.at[n], d_y)

    fcs = [fcopy(3, e)]
    fcs[0].start()
    for n in (2, 0, 1):
        q = targets[n]
        ocopy(n, q).wait_recv()
        fc = fcopy(n, q)
        fc.start()
        fcs.append(fc)

    def lwait(q):
        rcopy(LE.at[q], LE.at[q], l_send.at[0], l_recv.at[q], d_part).wait_recv()

    for ee in (part, xn, xp):
        lwait(ee)
    acc = LE[0]
    for b in range(1, n_e):
        acc = acc + LE[b]
    LI[i] = acc
    li = rcopy(LI.at[i], LI.at[i], l_send.at[3], l_recv.at[n_e], d_y)
    li.start()

    for s in range(1, n_c):
        cz = lax.rem(c + s, n_c)
        rcopy(ZS.at[cz], ZR.at[cz], z_send.at[cz], z_recv.at[cz], dev(i, cz, e)).wait_recv()
    dun = ZR[0]
    for b in range(1, n_c):
        dun = dun + ZR[b]
    r0 = pl.multiple_of(c * ch, ch)
    block = RG[i, pl.ds(r0, ch), :].astype(F32)
    inv = lax.rsqrt(jnp.sum(block * block, axis=1, keepdims=True) + 1e-06)
    unit = RG[i, pl.ds(r0, ch), cols(e)].astype(F32) * inv
    prod = unit * dun
    fold = prod[:, 0:128]
    for b in range(1, width // 128):
        fold = fold + prod[:, b * 128:(b + 1) * 128]
    rad = jnp.sum(fold.T, axis=0, keepdims=True)
    RD[e] = jnp.broadcast_to(rad, (8, ch))
    rcs = []
    for n, ee in enumerate((part, xn, xp)):
        rc = rcopy(RD.at[e], RD.at[e], r_send.at[n], r_recv.at[e], dev(i, c, ee))
        rc.start()
        rcs.append(rc)
    li.wait_recv()
    acc = LI[0]
    for b in range(1, n_i):
        acc = acc + LI[b]
    LC[c] = acc
    lz = []
    for s in range(1, n_c):
        q = rcopy(LC.at[c], LC.at[c], l_send.at[3 + s], l_recv.at[n_e + 1 + c], dev(i, lax.rem(c + s, n_c), e))
        q.start()
        lz.append(q)
    for ee in (part, xn, xp):
        rcopy(RD.at[ee], RD.at[ee], r_send.at[0], r_recv.at[ee], d_part).wait_recv()
    rsum = RD[0]
    for b in range(1, n_e):
        rsum = rsum + RD[b]
    radial = rsum.T[:, 0:1]
    RO[...] = (inv * (dun - unit * radial)).astype(BF16)
    wcs = []
    for s in range(1, n_c):
        q = rcopy(RO, rg_out.at[pl.ds(r0, ch), :], w_send.at[s - 1], w_recv.at[c], dev(i, lax.rem(c + s, n_c), e))
        q.start()
        wcs.append(q)
    own_r = pltpu.make_async_copy(RO, rg_out.at[pl.ds(r0, ch), :], loc.at[5])
    own_r.start()

    for s in range(1, n_c):
        cz = lax.rem(c + s, n_c)
        rcopy(LC.at[cz], LC.at[cz], l_send.at[4], l_recv.at[n_e + 1 + cz], dev(i, cz, e)).wait_recv()
    acc = LC[0]
    for b in range(1, n_c):
        acc = acc + LC[b]
    total = jnp.sum(jnp.sum(acc, axis=0, keepdims=True), axis=1, keepdims=True)
    loss_out[...] = jnp.broadcast_to(total / count / classes, (8, 128))

    for q in (own_x, own_y, own_p, sc_y, v_y, rel_p, rel_y, fy1, fy2):
        q.wait_send()
    for q in tcopies + lcs + [li] + lz + rcs + wcs + fcs:
        q.wait_send()
    for n in range(3):
        ocopy(n, targets[n]).wait_send()

    @pl.loop(0, n_t)
    def _(t):
        pcopy(t).wait_send()
        xcopy(t).wait_send()

        @pl.when(t < n_c)
        def _():
            ycopy(t).wait_send()

            @pl.when(t != c)
            def _():
                zcopy(t).wait_send()

    for n in range(4):
        rcopy(TS.at[n], tg_out.at[rblk(j), :], f_send.at[n], f_recv.at[n], d_y).wait_recv()
    for s in range(1, n_c):
        cz = lax.rem(c + s, n_c)
        rcopy(RO, rg_out.at[pl.ds(pl.multiple_of(cz * ch, ch), ch), :],
              w_send.at[s - 1], w_recv.at[cz], dev(i, cz, e)).wait_recv()
    own_o.wait()
    own_r.wait()


def fused(regions, table, shift, scale, labels, valid):
    n_i, n_c, n_e = (lax.axis_size(a) for a in ("img", "cls", "emb"))
    rows, width = regions.shape
    class_dev = table.shape[0]
    n_j = n_i * n_e
    blk = class_dev // n_j
    pad = -(-blk // 256) * 256
    ch = rows // n_c
    n_t = 2 * n_c
    imgs = valid.shape[0]
    full = n_e * width
    zero = jnp.zeros_like(shift)
    packed = jnp.stack([shift, scale, labels.astype(F32)] + [zero] * 5, axis=0)
    v = valid.astype(F32).reshape(imgs, n_j, blk).transpose(1, 0, 2)
    v = jnp.pad(v, ((0, 0), (0, 0), (0, pad - blk)))
    v = jnp.broadcast_to(v[:, :, None, :], (n_j, imgs, 8, pad))
    cfg = (n_i, n_c, n_e, rows, width, blk, pad, class_dev * n_c, imgs)
    dma = pltpu.SemaphoreType.DMA
    any_spec = pl.BlockSpec(memory_space=pl.ANY)
    loss, rg, tg = pl.pallas_call(
        functools.partial(kernel, cfg),
        out_shape=(
            jax.ShapeDtypeStruct((8, 128), F32),
            jax.ShapeDtypeStruct((rows, width), BF16),
            jax.ShapeDtypeStruct((class_dev, width), BF16),
        ),
        in_specs=[any_spec] * 4,
        out_specs=(pl.BlockSpec(memory_space=pltpu.VMEM), any_spec, any_spec),
        scratch_shapes=[
            pltpu.VMEM((n_i, rows, full), BF16),
            pltpu.VMEM((n_i * rows, full), BF16),
            pltpu.VMEM((pad, full), BF16),
            pltpu.VMEM((pad, n_i * rows), BF16),
            pltpu.VMEM((n_i, 8, rows), F32),
            pltpu.VMEM((n_i, imgs, 8, pad), F32),
            pltpu.VMEM((n_t, 2, ch, width), F32),
            pltpu.VMEM((n_t, 2, ch, width), F32),
            pltpu.VMEM((n_t, 2, ch, width), F32),
            pltpu.VMEM((n_t, ch, width), BF16),
            pltpu.VMEM((n_t, ch, width), BF16),
            pltpu.VMEM((n_c, ch, width), BF16),
            pltpu.VMEM((n_c, ch, width), BF16),
            pltpu.VMEM((n_c, ch, width), F32),
            pltpu.VMEM((n_c, ch, width), F32),
            pltpu.VMEM((4, blk, width), BF16),
            pltpu.VMEM((8, pad), F32),
            pltpu.VMEM((n_e, 8, 128), F32),
            pltpu.VMEM((n_i, 8, 128), F32),
            pltpu.VMEM((n_c, 8, 128), F32),
            pltpu.VMEM((n_e, 8, ch), F32),
            pltpu.VMEM((ch, width), BF16),
            dma((6,)), dma((7,)), dma((7,)), dma((3,)), dma((3,)), dma((2,)), dma((2,)),
            dma((n_t,)), dma((n_t,)), dma((n_t,)), dma((n_t,)),
            dma((n_c,)), dma((n_c,)), dma((n_c,)), dma((n_c,)),
            dma((4,)), dma((4,)), dma((4,)), dma((4,)),
            dma((4 + n_c,)), dma((n_e + 1 + n_c,)), dma((3,)), dma((n_e,)),
            dma((n_c,)), dma((n_c,)),
        ],
        compiler_params=pltpu.CompilerParams(
            collective_id=0, has_side_effects=True, vmem_limit_bytes=60000 * 1024),
    )(regions, table, packed, v)
    return loss[0, 0], rg, tg


def focal(logit, target):
    prob = jax.nn.sigmoid(logit)
    return -0.25 * target * (1.0 - prob) ** 2 * jax.nn.log_sigmoid(logit) - 0.75 * (
        1.0 - target
    ) * prob**2 * jax.nn.log_sigmoid(-logit)


def generic(regions, table, shift, scale, labels, valid):
    rows = regions.shape[0]
    class_dev = table.shape[0]
    parts = lax.axis_size("emb")
    quarter = rows // parts
    start = lax.axis_index("emb") * quarter
    block = regions.astype(jnp.float32)
    squares = lax.psum(jnp.sum(block * block, axis=1), "emb")
    local_count = jnp.sum((labels >= 0).astype(jnp.float32))
    count = lax.psum(local_count, "img")
    inv = lax.rsqrt(squares + 1e-06)
    unit = block * inv[:, None]
    unit_b = unit.astype(jnp.bfloat16)
    unit_rows = lax.all_to_all(unit_b, "emb", split_axis=0, concat_axis=1, tiled=True)
    cosine = lax.dot_general(
        unit_rows,
        lax.all_gather(table, "emb", axis=1, tiled=True),
        (((1,), (1,)), ((), ())),
        preferred_element_type=jnp.float32,
    )
    shift_q = lax.dynamic_slice_in_dim(shift, start, quarter, 0)
    scale_q = lax.dynamic_slice_in_dim(scale, start, quarter, 0)
    label_q = lax.dynamic_slice_in_dim(labels, start, quarter, 0)
    image_ids = (start + jnp.arange(quarter, dtype=jnp.int32)) // (rows // valid.shape[0])
    onehot = (image_ids[:, None] == jnp.arange(valid.shape[0], dtype=jnp.int32)[None, :]).astype(
        jnp.float32
    )
    mask = jnp.dot(onehot, valid.astype(jnp.float32), preferred_element_type=jnp.float32)
    class_ids = lax.axis_index("cls") * class_dev + jnp.arange(class_dev, dtype=jnp.int32)
    logit = (cosine + shift_q[:, None]) * scale_q[:, None]
    target = (label_q[:, None] == class_ids[None, :]).astype(jnp.float32)
    term, pullback = jax.vjp(lambda value: focal(value, target), logit)
    dlogit = pullback(jnp.ones_like(term))[0]
    total = lax.psum(jnp.sum(term * mask), ("img", "cls", "emb"))
    factor = rows * lax.axis_size("img") / count
    dscore = (dlogit * mask * scale_q[:, None] * factor).astype(jnp.bfloat16)
    piece = lax.all_gather(dscore, "emb", axis=0, tiled=True)
    dunit_piece = jnp.dot(piece, table, preferred_element_type=jnp.float32)
    table_acc = lax.dot_general(
        piece, unit_b, (((0,), (0,)), ((), ())), preferred_element_type=jnp.float32
    )
    dunit = lax.psum(dunit_piece, "cls")
    radial = lax.psum(jnp.sum(unit * dunit, axis=1), "emb")
    region_grad = (inv[:, None] * (dunit - unit * radial[:, None])).astype(jnp.bfloat16)
    table_grad = lax.psum(table_acc, "img").astype(jnp.bfloat16)
    loss = total / count / (class_dev * lax.axis_size("cls"))
    return (loss, region_grad, table_grad)


def shards(*args):
    n_i, n_c, n_e = (lax.axis_size(a) for a in ("img", "cls", "emb"))
    rows, width = args[0].shape
    class_dev = args[1].shape[0]
    per_img = rows // args[5].shape[0]
    fits = n_i == 2 and n_e == 4 and class_dev % (16 * n_i * n_e) == 0
    fits = fits and rows % (128 * n_c) == 0 and per_img % (rows // n_c) == 0
    fits = fits and width == 256
    return fused(*args) if fits else generic(*args)


def solution(mesh):
    placed = (P("img", "emb"), P("cls", "emb"), P("img"), P("img"), P("img"), P("img", "cls"))
    return jax.shard_map(
        shards,
        mesh=mesh,
        in_specs=placed,
        out_specs=(P(), P("img", "emb"), P("cls", "emb")),
        check_vma=False,
    )
```

```python
import functools

import jax
import jax.numpy as jnp
from jax import lax
from jax.experimental import pallas as pl
from jax.experimental.pallas import tpu as pltpu
from jax.sharding import PartitionSpec as P

MESH = pl.DeviceIdType.MESH
F32 = jnp.float32
BF16 = jnp.bfloat16


def kernel(cfg, regions, table, shift_in, scale_in, labels_in, valid, loss_out, rg_out, tg_out,
           RG, UN, TB, DS, SH, SL, LB, VB, SP, KP, PR, XS, XR, YS, YR, ZS, ZR, ZO,
           TS, LA, LE, LI, LC, RD, RO,
           loc, g_send, g_recv, gx_send, gx_recv, t_send, t_recv, s_send, s_recv,
           p_send, p_recv, x_send, x_recv, y_send, y_recv, z_send, z_recv,
           o_send, o_recv, f_send, f_recv, l_send, l_recv, r_send, r_recv,
           w_send, w_recv):
    n_i, n_c, n_e, rows, width, blk, pad, classes, imgs = cfg
    i, c, e = lax.axis_index("img"), lax.axis_index("cls"), lax.axis_index("emb")
    k = lax.rem(e, 2)
    x = e // 2
    oi = 1 - i
    part = 2 * x + 1 - k
    xn = 2 * (1 - x) + k
    xp = 2 * (1 - x) + 1 - k
    j = i * n_e + e
    ch = rows // n_c
    n_t = 2 * n_c
    full = n_e * width

    def dev(ii, cc, ee):
        return (ii, cc, ee)

    def rcopy(src, dst, ss, rs, d):
        return pltpu.make_async_remote_copy(
            src_ref=src, dst_ref=dst, send_sem=ss, recv_sem=rs,
            device_id=d, device_id_type=MESH)

    def cols(q):
        return pl.ds(pl.multiple_of(q * width, width), width)

    def rblk(q):
        return pl.ds(pl.multiple_of(q * blk, 16), blk)

    barrier = pltpu.get_barrier_semaphore()
    for ee in (part, xn, xp):
        pl.semaphore_signal(barrier, inc=1, device_id=dev(i, c, ee), device_id_type=MESH)
    pl.semaphore_signal(barrier, inc=1, device_id=dev(oi, c, e), device_id_type=MESH)
    for s in range(1, n_c):
        pl.semaphore_signal(barrier, inc=1, device_id=dev(i, lax.rem(c + s, n_c), e), device_id_type=MESH)
    pl.semaphore_wait(barrier, 3 + 1 + n_c - 1)

    d_part, d_xn, d_xp, d_y = dev(i, c, part), dev(i, c, xn), dev(i, c, xp), dev(oi, c, e)

    def rslice(im, m, q):
        return RG.at[im, pl.ds(pl.multiple_of(m * ch, ch), ch), cols(q)]

    def xin(m):
        return rcopy(regions.at[pl.ds(pl.multiple_of(m * ch, ch), ch), :], rslice(i, m, e),
                     gx_send.at[0, m], gx_recv.at[0, m], d_xn)

    def xin_wait(m):
        rcopy(rslice(i, m, xn), rslice(i, m, xn), gx_send.at[0, m], gx_recv.at[0, m], d_xn).wait_recv()

    def rel_y(m):
        return rcopy(rslice(i, m, xn), rslice(i, m, xn), gx_send.at[1, m], gx_recv.at[1, m], d_y)

    def rel_p(m):
        return rcopy(rslice(i, m, xn), rslice(i, m, xn), gx_send.at[2, m], gx_recv.at[2, m], d_part)

    def fwd_p(m):
        return rcopy(rslice(oi, m, xn), rslice(oi, m, xn), gx_send.at[3, m], gx_recv.at[3, m], d_part)

    def serve_x(m):
        xin_wait(m)
        rel_y(m).start()
        rel_p(m).start()

    def serve_y(m):
        rel_y(m).wait_recv()
        fwd_p(m).start()

    tcopies = []
    for n, ee in enumerate((xn, xp, part)):
        t = rcopy(table.at[rblk(i * n_e + ee), :], TB.at[pl.ds(0, blk), cols(e)],
                  t_send.at[n], t_recv.at[n], dev(i, c, ee))
        t.start()
        tcopies.append(t)
    smalls = []
    for n, (src, dst) in enumerate(((shift_in, SH), (scale_in, SL), (labels_in, LB),
                                    (valid.at[oi * n_e + e], VB))):
        q = rcopy(src, dst.at[i], s_send.at[n], s_recv.at[n], d_y)
        q.start()
        smalls.append(q)
    own_y = rcopy(regions, RG.at[i, :, cols(e)], g_send.at[0], g_recv.at[0], d_y)
    own_p = rcopy(regions, RG.at[i, :, cols(e)], g_send.at[1], g_recv.at[1], d_part)
    own_y.start()
    own_p.start()
    for m in range(n_c):
        xin(m).start()
    locs = [
        pltpu.make_async_copy(regions, RG.at[i, :, cols(e)], loc.at[0]),
        pltpu.make_async_copy(table.at[rblk(j), :], TB.at[pl.ds(0, blk), cols(e)], loc.at[1]),
        pltpu.make_async_copy(shift_in, SH.at[i], loc.at[2]),
        pltpu.make_async_copy(scale_in, SL.at[i], loc.at[3]),
        pltpu.make_async_copy(labels_in, LB.at[i], loc.at[6]),
        pltpu.make_async_copy(valid.at[j], VB.at[i], loc.at[7]),
    ]
    for q in locs:
        q.start()
    if pad > blk:
        TB[pl.ds(blk, pad - blk), :] = jnp.zeros((pad - blk, full), BF16)
    LA[...] = jnp.zeros_like(LA)

    own_y.wait_recv()
    fy1 = rcopy(RG.at[oi, :, cols(e)], RG.at[oi, :, cols(e)], g_send.at[2], g_recv.at[2], d_part)
    fy1.start()
    for q in locs:
        q.wait()
    for q in smalls:
        q.wait_recv()
    own_p.wait_recv()
    for t in tcopies:
        t.wait_recv()
    fy1.wait_recv()
    serve_x(0)

    fg = (LB[0] >= 0).astype(F32)
    for b in range(1, n_i):
        fg = fg + (LB[b] >= 0).astype(F32)
    count = jnp.sum(jnp.sum(fg, axis=0, keepdims=True), axis=1, keepdims=True)
    factor = (rows * n_i) / count

    base = (c * (n_i * n_e) + j) * blk
    class_ids = base + lax.broadcasted_iota(jnp.int32, (1, pad), 1)
    per_img = rows // imgs

    def column(ref, im, m):
        parts = []
        for b in range(ch // 128):
            row = ref[im, pl.ds(m * (ch // 128) + b, 1), :]
            parts.append(jnp.broadcast_to(row, (8, 128)).T[:, 0:1])
        return jnp.concatenate(parts, axis=0)

    def pcopy(t):
        return rcopy(SP.at[t], PR.at[t], p_send.at[t], p_recv.at[t], d_part)

    def xcopy(t):
        return rcopy(XS.at[t], XR.at[t], x_send.at[t], x_recv.at[t], d_xn)

    def ycopy(t):
        return rcopy(YS.at[t], YR.at[t], y_send.at[t], y_recv.at[t], d_y)

    def zcopy(m):
        return rcopy(ZS.at[m], ZR.at[c], z_send.at[m], z_recv.at[c], dev(i, m, e))

    def compute(im, m, t):
        r0 = pl.multiple_of(m * ch, ch)
        block = RG[im, pl.ds(r0, ch), :].astype(F32)
        inv = lax.rsqrt(jnp.sum(block * block, axis=1, keepdims=True) + 1e-06)
        unit_b = (block * inv).astype(BF16)
        u0 = pl.multiple_of(im * rows + m * ch, ch)
        UN[pl.ds(u0, ch), :] = unit_b
        cosine = lax.dot_general(unit_b, TB[...], (((1,), (1,)), ((), ())),
                                 preferred_element_type=F32)
        shift, scale, label = column(SH, im, m), column(SL, im, m), column(LB, im, m)
        mask = VB[im, (m * ch) // per_img][0:1, :]
        z = (cosine + shift) * scale
        hit = label == class_ids
        s = jnp.where(hit, -z, z)
        ex = jnp.exp(-jnp.abs(s))
        den = 1.0 + ex
        r = 1.0 / den
        er = ex * r
        pos = s >= 0
        q = jnp.where(pos, r, er)
        nq = jnp.where(pos, er, r)
        lg = jnp.where(ex < 0.01, ex * (1.0 - ex * (0.5 - ex * (1.0 / 3.0))), jnp.log(den))
        soft = jnp.maximum(s, 0.0) + lg
        wq = jnp.where(hit, 0.25, 0.75) * (q * q) * mask
        term = wq * soft
        LA[...] += jnp.sum(term.reshape(ch // 8, 8, pad), axis=0)
        g = wq * (q + 2.0 * nq * soft)
        g = jnp.where(hit, -g, g) * (scale * factor)
        ds = g.astype(BF16)
        DS[:, pl.ds(u0, ch)] = ds.T
        for xi in range(2):
            SP[t, xi] = jnp.dot(ds, TB[:, cols(2 * xi + 1 - k)], preferred_element_type=F32)
            KP[t, xi] = jnp.dot(ds, TB[:, cols(2 * xi + k)], preferred_element_type=F32)
        pcopy(t).start()

    def stage2(t):
        pcopy(t).wait_recv()
        XS[t] = (KP[t, 1 - x] + PR[t, 1 - x]).astype(BF16)
        xcopy(t).start()
        KP[t, x] = KP[t, x] + PR[t, x]

    def stage3_other(m):
        t = 2 * m + 1
        xcopy(t).wait_recv()
        YS[m] = (KP[t, x] + XR[t].astype(F32)).astype(BF16)
        ycopy(m).start()

    def stage3_own(m):
        t = 2 * m
        xcopy(t).wait_recv()
        val = KP[t, x] + XR[t].astype(F32)
        ycopy(m).wait_recv()
        tot = val + YR[m].astype(F32)

        @pl.when(m == c)
        def _():
            ZO[...] = tot

        @pl.when(m != c)
        def _():
            ZS[m] = tot.astype(BF16)
            zcopy(m).start()

    @pl.loop(0, n_c)
    def _(m):
        @pl.when(m + 1 < n_c)
        def _():
            serve_x(m + 1)

        rel_p(m).wait_recv()
        compute(i, m, 2 * m)
        serve_y(m)

        @pl.when(m >= 1)
        def _():
            stage2(2 * m - 1)

        fwd_p(m).wait_recv()
        compute(oi, m, 2 * m + 1)
        stage2(2 * m)

        @pl.when(m >= 2)
        def _():
            stage3_other(m - 2)

        @pl.when(m >= 3)
        def _():
            stage3_own(m - 3)

    tile = LA[:, 0:128]
    for b in range(1, pad // 128):
        tile = tile + LA[:, b * 128:(b + 1) * 128]
    LI[i] = tile
    li = rcopy(LI.at[i], LI.at[i], l_send.at[0], l_recv.at[0], d_y)
    li.start()
    stage2(n_t - 1)

    def ocopy(n, q):
        return rcopy(TS.at[n], tg_out.at[rblk(j), :], o_send.at[n], o_recv.at[n], dev(i, c, q))

    targets = (xn, xp, part, e)
    dst_of = []

    def tg_of(n, q):
        TS[n] = jnp.dot(DS[0:blk, :], UN[:, cols(q)], preferred_element_type=F32).astype(BF16)

    @pl.loop(0, 4)
    def _(n):
        xx = jnp.where(n < 2, 1 - x, x)
        kk = jnp.where((n == 0) | (n == 3), k, 1 - k)
        q = 2 * xx + kk
        tg_of(n, q)

        @pl.when(n < 3)
        def _():
            ocopy(n, q).start()

    own_o = pltpu.make_async_copy(TS.at[3], tg_out.at[rblk(j), :], loc.at[4])
    own_o.start()

    def fcopy(n, q):
        src = TS.at[3] if n == 3 else tg_out.at[rblk(i * n_e + q), :]
        return rcopy(src, tg_out.at[rblk(i * n_e + q), :], f_send.at[n], f_recv.at[n], d_y)

    first_other = max(n_c - 2, 0)
    first_own = max(n_c - 3, 0)
    for m in range(first_other, n_c):
        stage3_other(m)
    li.wait_recv()
    acc = LI[0]
    for b in range(1, n_i):
        acc = acc + LI[b]
    LC[c] = acc
    lz = []
    for s in range(1, n_c):
        q = rcopy(LC.at[c], LC.at[c], l_send.at[s], l_recv.at[1 + c], dev(i, lax.rem(c + s, n_c), e))
        q.start()
        lz.append(q)
    for m in range(first_own, n_c):
        stage3_own(m)
    fcs = [fcopy(3, e)]
    fcs[0].start()
    for n in (2, 0, 1):
        q = targets[n]
        ocopy(n, q).wait_recv()
        fc = fcopy(n, q)
        fc.start()
        fcs.append(fc)

    for s in range(1, n_c):
        cz = lax.rem(c + s, n_c)
        rcopy(LC.at[cz], LC.at[cz], l_send.at[1], l_recv.at[1 + cz], dev(i, cz, e)).wait_recv()
    acc = LC[0]
    for b in range(1, n_c):
        acc = acc + LC[b]
    LE[e] = acc
    lcs = []
    for n, ee in enumerate((part, xn, xp)):
        lc = rcopy(LE.at[e], LE.at[e], l_send.at[n_c + n], l_recv.at[1 + n_c + e], dev(i, c, ee))
        lc.start()
        lcs.append(lc)

    for s in range(1, n_c):
        cz = lax.rem(c + s, n_c)
        rcopy(ZS.at[cz], ZR.at[cz], z_send.at[cz], z_recv.at[cz], dev(i, cz, e)).wait_recv()
    dun = ZO[...]
    for s in range(1, n_c):
        dun = dun + ZR[lax.rem(c + s, n_c)].astype(F32)
    r0 = pl.multiple_of(c * ch, ch)
    block = RG[i, pl.ds(r0, ch), :].astype(F32)
    inv = lax.rsqrt(jnp.sum(block * block, axis=1, keepdims=True) + 1e-06)
    unit = RG[i, pl.ds(r0, ch), cols(e)].astype(F32) * inv
    prod = unit * dun
    fold = prod[:, 0:128]
    for b in range(1, width // 128):
        fold = fold + prod[:, b * 128:(b + 1) * 128]
    rad = jnp.sum(fold.T, axis=0, keepdims=True)
    RD[e] = jnp.broadcast_to(rad, (8, ch))
    rcs = []
    for n, ee in enumerate((part, xn, xp)):
        rc = rcopy(RD.at[e], RD.at[e], r_send.at[n], r_recv.at[e], dev(i, c, ee))
        rc.start()
        rcs.append(rc)
    for ee in (part, xn, xp):
        rcopy(RD.at[ee], RD.at[ee], r_send.at[0], r_recv.at[ee], d_part).wait_recv()
    rsum = RD[0]
    for b in range(1, n_e):
        rsum = rsum + RD[b]
    radial = rsum.T[:, 0:1]
    RO[...] = (inv * (dun - unit * radial)).astype(BF16)
    wcs = []
    for s in range(1, n_c):
        q = rcopy(RO, rg_out.at[pl.ds(r0, ch), :], w_send.at[s - 1], w_recv.at[c], dev(i, lax.rem(c + s, n_c), e))
        q.start()
        wcs.append(q)
    own_r = pltpu.make_async_copy(RO, rg_out.at[pl.ds(r0, ch), :], loc.at[5])
    own_r.start()

    for ee in (part, xn, xp):
        rcopy(LE.at[ee], LE.at[ee], l_send.at[n_c], l_recv.at[1 + n_c + ee], d_part).wait_recv()
    acc = LE[0]
    for b in range(1, n_e):
        acc = acc + LE[b]
    total = jnp.sum(jnp.sum(acc, axis=0, keepdims=True), axis=1, keepdims=True)
    loss_out[...] = jnp.broadcast_to(total / count / classes, (8, 128))

    for q in [own_y, own_p, fy1] + smalls + tcopies + lcs + [li] + lz + rcs + wcs + fcs:
        q.wait_send()
    for n in range(3):
        ocopy(n, targets[n]).wait_send()

    @pl.loop(0, n_t)
    def _(t):
        pcopy(t).wait_send()
        xcopy(t).wait_send()

        @pl.when(t < n_c)
        def _():
            xin(t).wait_send()
            rel_y(t).wait_send()
            rel_p(t).wait_send()
            fwd_p(t).wait_send()
            ycopy(t).wait_send()

            @pl.when(t != c)
            def _():
                zcopy(t).wait_send()

    for n in range(4):
        rcopy(TS.at[n], tg_out.at[rblk(j), :], f_send.at[n], f_recv.at[n], d_y).wait_recv()
    for s in range(1, n_c):
        cz = lax.rem(c + s, n_c)
        rcopy(RO, rg_out.at[pl.ds(pl.multiple_of(cz * ch, ch), ch), :],
              w_send.at[s - 1], w_recv.at[cz], dev(i, cz, e)).wait_recv()
    own_o.wait()
    own_r.wait()


def fused(regions, table, shift, scale, labels, valid):
    n_i, n_c, n_e = (lax.axis_size(a) for a in ("img", "cls", "emb"))
    rows, width = regions.shape
    class_dev = table.shape[0]
    n_j = n_i * n_e
    blk = class_dev // n_j
    pad = -(-blk // 256) * 256
    ch = rows // n_c
    n_t = 2 * n_c
    imgs = valid.shape[0]
    full = n_e * width
    lanes = (rows // 128, 128)
    v = valid.astype(F32).reshape(imgs, n_j, blk).transpose(1, 0, 2)
    v = jnp.pad(v, ((0, 0), (0, 0), (0, pad - blk)))
    v = jnp.broadcast_to(v[:, :, None, :], (n_j, imgs, 8, pad))
    cfg = (n_i, n_c, n_e, rows, width, blk, pad, class_dev * n_c, imgs)
    dma = pltpu.SemaphoreType.DMA
    any_spec = pl.BlockSpec(memory_space=pl.ANY)
    loss, rg, tg = pl.pallas_call(
        functools.partial(kernel, cfg),
        out_shape=(
            jax.ShapeDtypeStruct((8, 128), F32),
            jax.ShapeDtypeStruct((rows, width), BF16),
            jax.ShapeDtypeStruct((class_dev, width), BF16),
        ),
        in_specs=[any_spec] * 6,
        out_specs=(pl.BlockSpec(memory_space=pltpu.VMEM), any_spec, any_spec),
        scratch_shapes=[
            pltpu.VMEM((n_i, rows, full), BF16),
            pltpu.VMEM((n_i * rows, full), BF16),
            pltpu.VMEM((pad, full), BF16),
            pltpu.VMEM((pad, n_i * rows), BF16),
            pltpu.VMEM((n_i,) + lanes, F32),
            pltpu.VMEM((n_i,) + lanes, F32),
            pltpu.VMEM((n_i,) + lanes, jnp.int32),
            pltpu.VMEM((n_i, imgs, 8, pad), F32),
            pltpu.VMEM((n_t, 2, ch, width), F32),
            pltpu.VMEM((n_t, 2, ch, width), F32),
            pltpu.VMEM((n_t, 2, ch, width), F32),
            pltpu.VMEM((n_t, ch, width), BF16),
            pltpu.VMEM((n_t, ch, width), BF16),
            pltpu.VMEM((n_c, ch, width), BF16),
            pltpu.VMEM((n_c, ch, width), BF16),
            pltpu.VMEM((n_c, ch, width), BF16),
            pltpu.VMEM((n_c, ch, width), BF16),
            pltpu.VMEM((ch, width), F32),
            pltpu.VMEM((4, blk, width), BF16),
            pltpu.VMEM((8, pad), F32),
            pltpu.VMEM((n_e, 8, 128), F32),
            pltpu.VMEM((n_i, 8, 128), F32),
            pltpu.VMEM((n_c, 8, 128), F32),
            pltpu.VMEM((n_e, 8, ch), F32),
            pltpu.VMEM((ch, width), BF16),
            dma((8,)), dma((3,)), dma((3,)), dma((4, n_c)), dma((4, n_c)),
            dma((3,)), dma((3,)), dma((4,)), dma((4,)),
            dma((n_t,)), dma((n_t,)), dma((n_t,)), dma((n_t,)),
            dma((n_c,)), dma((n_c,)), dma((n_c,)), dma((n_c,)),
            dma((4,)), dma((4,)), dma((4,)), dma((4,)),
            dma((n_c + 3,)), dma((1 + n_c + n_e,)), dma((3,)), dma((n_e,)),
            dma((n_c,)), dma((n_c,)),
        ],
        compiler_params=pltpu.CompilerParams(
            collective_id=0, has_side_effects=True, vmem_limit_bytes=60000 * 1024),
    )(regions, table, shift.reshape(lanes), scale.reshape(lanes), labels.reshape(lanes), v)
    return loss[0, 0], rg, tg


def focal(logit, target):
    prob = jax.nn.sigmoid(logit)
    return -0.25 * target * (1.0 - prob) ** 2 * jax.nn.log_sigmoid(logit) - 0.75 * (
        1.0 - target
    ) * prob**2 * jax.nn.log_sigmoid(-logit)


def generic(regions, table, shift, scale, labels, valid):
    rows = regions.shape[0]
    class_dev = table.shape[0]
    parts = lax.axis_size("emb")
    quarter = rows // parts
    start = lax.axis_index("emb") * quarter
    block = regions.astype(jnp.float32)
    squares = lax.psum(jnp.sum(block * block, axis=1), "emb")
    local_count = jnp.sum((labels >= 0).astype(jnp.float32))
    count = lax.psum(local_count, "img")
    inv = lax.rsqrt(squares + 1e-06)
    unit = block * inv[:, None]
    unit_b = unit.astype(jnp.bfloat16)
    unit_rows = lax.all_to_all(unit_b, "emb", split_axis=0, concat_axis=1, tiled=True)
    cosine = lax.dot_general(
        unit_rows,
        lax.all_gather(table, "emb", axis=1, tiled=True),
        (((1,), (1,)), ((), ())),
        preferred_element_type=jnp.float32,
    )
    shift_q = lax.dynamic_slice_in_dim(shift, start, quarter, 0)
    scale_q = lax.dynamic_slice_in_dim(scale, start, quarter, 0)
    label_q = lax.dynamic_slice_in_dim(labels, start, quarter, 0)
    image_ids = (start + jnp.arange(quarter, dtype=jnp.int32)) // (rows // valid.shape[0])
    onehot = (image_ids[:, None] == jnp.arange(valid.shape[0], dtype=jnp.int32)[None, :]).astype(
        jnp.float32
    )
    mask = jnp.dot(onehot, valid.astype(jnp.float32), preferred_element_type=jnp.float32)
    class_ids = lax.axis_index("cls") * class_dev + jnp.arange(class_dev, dtype=jnp.int32)
    logit = (cosine + shift_q[:, None]) * scale_q[:, None]
    target = (label_q[:, None] == class_ids[None, :]).astype(jnp.float32)
    term, pullback = jax.vjp(lambda value: focal(value, target), logit)
    dlogit = pullback(jnp.ones_like(term))[0]
    total = lax.psum(jnp.sum(term * mask), ("img", "cls", "emb"))
    factor = rows * lax.axis_size("img") / count
    dscore = (dlogit * mask * scale_q[:, None] * factor).astype(jnp.bfloat16)
    piece = lax.all_gather(dscore, "emb", axis=0, tiled=True)
    dunit_piece = jnp.dot(piece, table, preferred_element_type=jnp.float32)
    table_acc = lax.dot_general(
        piece, unit_b, (((0,), (0,)), ((), ())), preferred_element_type=jnp.float32
    )
    dunit = lax.psum(dunit_piece, "cls")
    radial = lax.psum(jnp.sum(unit * dunit, axis=1), "emb")
    region_grad = (inv[:, None] * (dunit - unit * radial[:, None])).astype(jnp.bfloat16)
    table_grad = lax.psum(table_acc, "img").astype(jnp.bfloat16)
    loss = total / count / (class_dev * lax.axis_size("cls"))
    return (loss, region_grad, table_grad)


def shards(*args):
    n_i, n_c, n_e = (lax.axis_size(a) for a in ("img", "cls", "emb"))
    rows, width = args[0].shape
    class_dev = args[1].shape[0]
    per_img = rows // args[5].shape[0]
    fits = n_i == 2 and n_e == 4 and class_dev % (16 * n_i * n_e) == 0
    fits = fits and rows % (128 * n_c) == 0 and per_img % (rows // n_c) == 0
    fits = fits and width == 256
    return fused(*args) if fits else generic(*args)


def solution(mesh):
    placed = (P("img", "emb"), P("cls", "emb"), P("img"), P("img"), P("img"), P("img", "cls"))
    return jax.shard_map(
        shards,
        mesh=mesh,
        in_specs=placed,
        out_specs=(P(), P("img", "emb"), P("cls", "emb")),
        check_vma=False,
    )
```

```python
import functools

import jax
import jax.numpy as jnp
from jax import lax
from jax.experimental import pallas as pl
from jax.experimental.pallas import tpu as pltpu
from jax.sharding import PartitionSpec as P

MESH = pl.DeviceIdType.MESH
F32 = jnp.float32
BF16 = jnp.bfloat16


def kernel(cfg, regions, table, shift_in, scale_in, labels_in, valid, loss_out, rg_out, tg_out,
           RG, UN, TB, DS, SH, SL, LB, VB, SP, KP, PR, XS, XR, YS, YR, ZS, ZR, ZO,
           TS, LA, LE, LI, LC, RD, RO,
           loc, g_send, g_recv, gx_send, gx_recv, t_send, t_recv, s_send, s_recv,
           p_send, p_recv, x_send, x_recv, y_send, y_recv, z_send, z_recv,
           o_send, o_recv, f_send, f_recv, l_send, l_recv, r_send, r_recv,
           w_send, w_recv):
    n_i, n_c, n_e, rows, width, blk, pad, classes, imgs = cfg
    i, c, e = lax.axis_index("img"), lax.axis_index("cls"), lax.axis_index("emb")
    k = lax.rem(e, 2)
    x = e // 2
    oi = 1 - i
    part = 2 * x + 1 - k
    xn = 2 * (1 - x) + k
    xp = 2 * (1 - x) + 1 - k
    j = i * n_e + e
    ch = rows // n_c
    n_t = 2 * n_c
    full = n_e * width

    def dev(ii, cc, ee):
        return (ii, cc, ee)

    def rcopy(src, dst, ss, rs, d):
        return pltpu.make_async_remote_copy(
            src_ref=src, dst_ref=dst, send_sem=ss, recv_sem=rs,
            device_id=d, device_id_type=MESH)

    def cols(q):
        return pl.ds(pl.multiple_of(q * width, width), width)

    def rblk(q):
        return pl.ds(pl.multiple_of(q * blk, 16), blk)

    barrier = pltpu.get_barrier_semaphore()
    for ee in (part, xn, xp):
        pl.semaphore_signal(barrier, inc=1, device_id=dev(i, c, ee), device_id_type=MESH)
    pl.semaphore_signal(barrier, inc=1, device_id=dev(oi, c, e), device_id_type=MESH)
    for s in range(1, n_c):
        pl.semaphore_signal(barrier, inc=1, device_id=dev(i, lax.rem(c + s, n_c), e), device_id_type=MESH)
    pl.semaphore_wait(barrier, 3 + 1 + n_c - 1)

    d_part, d_xn, d_xp, d_y = dev(i, c, part), dev(i, c, xn), dev(i, c, xp), dev(oi, c, e)

    def rslice(im, m, q):
        return RG.at[im, pl.ds(pl.multiple_of(m * ch, ch), ch), cols(q)]

    def xin(m):
        return rcopy(regions.at[pl.ds(pl.multiple_of(m * ch, ch), ch), :], rslice(i, m, e),
                     gx_send.at[0, m], gx_recv.at[0, m], d_xn)

    def xin_wait(m):
        rcopy(rslice(i, m, xn), rslice(i, m, xn), gx_send.at[0, m], gx_recv.at[0, m], d_xn).wait_recv()

    def rel_y(m):
        return rcopy(rslice(i, m, xn), rslice(i, m, xn), gx_send.at[1, m], gx_recv.at[1, m], d_y)

    def rel_p(m):
        return rcopy(rslice(i, m, xn), rslice(i, m, xn), gx_send.at[2, m], gx_recv.at[2, m], d_part)

    def fwd_p(m):
        return rcopy(rslice(oi, m, xn), rslice(oi, m, xn), gx_send.at[3, m], gx_recv.at[3, m], d_part)

    def serve_x(m):
        xin_wait(m)
        rel_y(m).start()
        rel_p(m).start()

    def serve_y(m):
        rel_y(m).wait_recv()
        fwd_p(m).start()

    tcopies = []
    for n, ee in enumerate((xn, xp, part)):
        t = rcopy(table.at[rblk(i * n_e + ee), :], TB.at[pl.ds(0, blk), cols(e)],
                  t_send.at[n], t_recv.at[n], dev(i, c, ee))
        t.start()
        tcopies.append(t)
    smalls = []
    for n, (src, dst) in enumerate(((shift_in, SH), (scale_in, SL), (labels_in, LB),
                                    (valid.at[oi * n_e + e], VB))):
        q = rcopy(src, dst.at[i], s_send.at[n], s_recv.at[n], d_y)
        q.start()
        smalls.append(q)
    own_y = rcopy(regions, RG.at[i, :, cols(e)], g_send.at[0], g_recv.at[0], d_y)
    own_p = rcopy(regions, RG.at[i, :, cols(e)], g_send.at[1], g_recv.at[1], d_part)
    own_y.start()
    own_p.start()
    for m in range(n_c):
        xin(m).start()
    locs = [
        pltpu.make_async_copy(regions, RG.at[i, :, cols(e)], loc.at[0]),
        pltpu.make_async_copy(table.at[rblk(j), :], TB.at[pl.ds(0, blk), cols(e)], loc.at[1]),
        pltpu.make_async_copy(shift_in, SH.at[i], loc.at[2]),
        pltpu.make_async_copy(scale_in, SL.at[i], loc.at[3]),
        pltpu.make_async_copy(labels_in, LB.at[i], loc.at[6]),
        pltpu.make_async_copy(valid.at[j], VB.at[i], loc.at[7]),
    ]
    for q in locs:
        q.start()
    if pad > blk:
        TB[pl.ds(blk, pad - blk), :] = jnp.zeros((pad - blk, full), BF16)
    LA[...] = jnp.zeros_like(LA)

    own_y.wait_recv()
    fy1 = rcopy(RG.at[oi, :, cols(e)], RG.at[oi, :, cols(e)], g_send.at[2], g_recv.at[2], d_part)
    fy1.start()
    for q in locs:
        q.wait()
    for q in smalls:
        q.wait_recv()
    own_p.wait_recv()
    for t in tcopies:
        t.wait_recv()
    fy1.wait_recv()
    serve_x(0)

    fg = (LB[0] >= 0).astype(F32)
    for b in range(1, n_i):
        fg = fg + (LB[b] >= 0).astype(F32)
    count = jnp.sum(jnp.sum(fg, axis=0, keepdims=True), axis=1, keepdims=True)
    factor = (rows * n_i) / count

    base = (c * (n_i * n_e) + j) * blk
    class_ids = base + lax.broadcasted_iota(jnp.int32, (1, pad), 1)
    per_img = rows // imgs

    def column(ref, im, m):
        parts = []
        for b in range(ch // 128):
            row = ref[im, pl.ds(m * (ch // 128) + b, 1), :]
            parts.append(jnp.broadcast_to(row, (8, 128)).T[:, 0:1])
        return jnp.concatenate(parts, axis=0)

    def pcopy(t):
        return rcopy(SP.at[t], PR.at[t], p_send.at[t], p_recv.at[t], d_part)

    def xcopy(t):
        return rcopy(XS.at[t], XR.at[t], x_send.at[t], x_recv.at[t], d_xn)

    def ycopy(t):
        return rcopy(YS.at[t], YR.at[t], y_send.at[t], y_recv.at[t], d_y)

    def zcopy(m):
        return rcopy(ZS.at[m], ZR.at[c], z_send.at[m], z_recv.at[c], dev(i, m, e))

    def compute(im, m, t):
        r0 = pl.multiple_of(m * ch, ch)
        block = RG[im, pl.ds(r0, ch), :].astype(F32)
        inv = lax.rsqrt(jnp.sum(block * block, axis=1, keepdims=True) + 1e-06)
        unit_b = (block * inv).astype(BF16)
        u0 = pl.multiple_of(im * rows + m * ch, ch)
        UN[pl.ds(u0, ch), :] = unit_b
        cosine = lax.dot_general(unit_b, TB[...], (((1,), (1,)), ((), ())),
                                 preferred_element_type=F32)
        shift, scale, label = column(SH, im, m), column(SL, im, m), column(LB, im, m)
        mask = VB[im, (m * ch) // per_img][0:1, :]
        z = (cosine + shift) * scale
        hit = label == class_ids
        s = jnp.where(hit, -z, z)
        ex = jnp.exp(-jnp.abs(s))
        den = 1.0 + ex
        r = 1.0 / den
        er = ex * r
        pos = s >= 0
        q = jnp.where(pos, r, er)
        nq = jnp.where(pos, er, r)
        lg = jnp.where(ex < 0.01, ex * (1.0 - ex * (0.5 - ex * (1.0 / 3.0))), jnp.log(den))
        soft = jnp.maximum(s, 0.0) + lg
        wq = jnp.where(hit, 0.25, 0.75) * (q * q) * mask
        term = wq * soft
        LA[...] += jnp.sum(term.reshape(ch // 8, 8, pad), axis=0)
        g = wq * (q + 2.0 * nq * soft)
        g = jnp.where(hit, -g, g) * (scale * factor)
        ds = g.astype(BF16)
        DS[:, pl.ds(u0, ch)] = ds.T
        for xi in range(2):
            SP[t, xi] = jnp.dot(ds, TB[:, cols(2 * xi + 1 - k)], preferred_element_type=F32).astype(BF16)
            KP[t, xi] = jnp.dot(ds, TB[:, cols(2 * xi + k)], preferred_element_type=F32)

    def stage2(t):
        pcopy(t).wait_recv()
        XS[t] = (KP[t, 1 - x] + PR[t, 1 - x].astype(F32)).astype(BF16)
        xcopy(t).start()
        KP[t, x] = KP[t, x] + PR[t, x].astype(F32)

    def ocopy(n, q):
        return rcopy(TS.at[n], tg_out.at[rblk(j), :], o_send.at[n], o_recv.at[n], dev(i, c, q))

    targets = (xn, xp, part, e)
    def tg_of(n, q):
        TS[n] = jnp.dot(DS[0:blk, :], UN[:, cols(q)], preferred_element_type=F32).astype(BF16)

    def fcopy(n, q):
        src = TS.at[3] if n == 3 else tg_out.at[rblk(i * n_e + q), :]
        return rcopy(src, tg_out.at[rblk(i * n_e + q), :], f_send.at[n], f_recv.at[n], d_y)

    def slot_own(m):
        return jnp.where(m < 2, m, 2 * m - 2)

    def slot_other(m):
        return jnp.where(m < n_c - 2, 2 * m + 3, m + n_c)

    def stage3_other(m):
        t = slot_other(m)
        xcopy(t).wait_recv()
        YS[m] = (KP[t, x] + XR[t].astype(F32)).astype(BF16)
        ycopy(m).start()

    def stage3_own(m):
        t = slot_own(m)
        xcopy(t).wait_recv()
        val = KP[t, x] + XR[t].astype(F32)
        ycopy(m).wait_recv()
        tot = val + YR[m].astype(F32)

        @pl.when(m == c)
        def _():
            ZO[...] = tot

        @pl.when(m != c)
        def _():
            ZS[m] = tot.astype(BF16)
            zcopy(m).start()

    @pl.loop(0, n_t)
    def _(t):
        late = t >= 2 * (n_c - 1)
        odd = lax.rem(t, 2) == 1
        is_other = late | (odd & (t >= 2))
        m = jnp.where(t < 2, t, jnp.where(late, t - n_c, jnp.where(odd, (t - 3) // 2, t // 2 + 1)))
        im = jnp.where(is_other, oi, i)

        @pl.when(is_other)
        def _():
            fwd_p(m).wait_recv()

        @pl.when(jnp.logical_not(is_other))
        def _():
            rel_p(m).wait_recv()

        compute(im, m, t)

        @pl.when((t >= 1) & (t <= n_c))
        def _():
            serve_y(t - 1)

        @pl.when(t + 1 < n_c)
        def _():
            serve_x(t + 1)

        pcopy(t).start()

        @pl.when(t >= 1)
        def _():
            stage2(t - 1)

        @pl.when(t == n_t - 2)
        def _():
            stage3_other(0)

    tg_of(3, e)
    own_f = fcopy(3, e)
    own_f.start()

    tile = LA[:, 0:128]
    for b in range(1, pad // 128):
        tile = tile + LA[:, b * 128:(b + 1) * 128]
    LI[i] = tile
    li = rcopy(LI.at[i], LI.at[i], l_send.at[0], l_recv.at[0], d_y)
    li.start()
    stage2(n_t - 1)

    @pl.loop(0, 3)
    def _(b):
        n = lax.rem(b + 2, 3)
        q = 2 * jnp.where(n < 2, 1 - x, x) + jnp.where(n == 0, k, 1 - k)
        tg_of(n, q)
        ocopy(n, q).start()

    own_o = pltpu.make_async_copy(TS.at[3], tg_out.at[rblk(j), :], loc.at[4])
    own_o.start()

    for m in range(1, n_c):
        stage3_other(m)
    li.wait_recv()
    acc = LI[0]
    for b in range(1, n_i):
        acc = acc + LI[b]
    LC[c] = acc
    lz = []
    for s in range(1, n_c):
        q = rcopy(LC.at[c], LC.at[c], l_send.at[s], l_recv.at[1 + c], dev(i, lax.rem(c + s, n_c), e))
        q.start()
        lz.append(q)
    for m in range(n_c):
        stage3_own(m)
    fcs = [own_f]
    for n in (2, 0, 1):
        q = targets[n]
        ocopy(n, q).wait_recv()
        fc = fcopy(n, q)
        fc.start()
        fcs.append(fc)

    for s in range(1, n_c):
        cz = lax.rem(c + s, n_c)
        rcopy(LC.at[cz], LC.at[cz], l_send.at[1], l_recv.at[1 + cz], dev(i, cz, e)).wait_recv()
    acc = LC[0]
    for b in range(1, n_c):
        acc = acc + LC[b]
    LE[e] = acc
    lcs = []
    for n, ee in enumerate((part, xn, xp)):
        lc = rcopy(LE.at[e], LE.at[e], l_send.at[n_c + n], l_recv.at[1 + n_c + e], dev(i, c, ee))
        lc.start()
        lcs.append(lc)

    for s in range(1, n_c):
        cz = lax.rem(c + s, n_c)
        rcopy(ZS.at[cz], ZR.at[cz], z_send.at[cz], z_recv.at[cz], dev(i, cz, e)).wait_recv()
    dun = ZO[...]
    for s in range(1, n_c):
        dun = dun + ZR[lax.rem(c + s, n_c)].astype(F32)
    r0 = pl.multiple_of(c * ch, ch)
    block = RG[i, pl.ds(r0, ch), :].astype(F32)
    inv = lax.rsqrt(jnp.sum(block * block, axis=1, keepdims=True) + 1e-06)
    unit = RG[i, pl.ds(r0, ch), cols(e)].astype(F32) * inv
    prod = unit * dun
    fold = prod[:, 0:128]
    for b in range(1, width // 128):
        fold = fold + prod[:, b * 128:(b + 1) * 128]
    rad = jnp.sum(fold.T, axis=0, keepdims=True)
    RD[e] = jnp.broadcast_to(rad, (8, ch))
    rcs = []
    for n, ee in enumerate((part, xn, xp)):
        rc = rcopy(RD.at[e], RD.at[e], r_send.at[n], r_recv.at[e], dev(i, c, ee))
        rc.start()
        rcs.append(rc)
    for ee in (part, xn, xp):
        rcopy(RD.at[ee], RD.at[ee], r_send.at[0], r_recv.at[ee], d_part).wait_recv()
    rsum = RD[0]
    for b in range(1, n_e):
        rsum = rsum + RD[b]
    radial = rsum.T[:, 0:1]
    RO[...] = (inv * (dun - unit * radial)).astype(BF16)
    wcs = []
    for s in range(1, n_c):
        q = rcopy(RO, rg_out.at[pl.ds(r0, ch), :], w_send.at[s - 1], w_recv.at[c], dev(i, lax.rem(c + s, n_c), e))
        q.start()
        wcs.append(q)
    own_r = pltpu.make_async_copy(RO, rg_out.at[pl.ds(r0, ch), :], loc.at[5])
    own_r.start()

    for ee in (part, xn, xp):
        rcopy(LE.at[ee], LE.at[ee], l_send.at[n_c], l_recv.at[1 + n_c + ee], d_part).wait_recv()
    acc = LE[0]
    for b in range(1, n_e):
        acc = acc + LE[b]
    total = jnp.sum(jnp.sum(acc, axis=0, keepdims=True), axis=1, keepdims=True)
    loss_out[...] = jnp.broadcast_to(total / count / classes, (8, 128))

    for q in [own_y, own_p, fy1] + smalls + tcopies + lcs + [li] + lz + rcs + wcs + fcs:
        q.wait_send()
    for n in range(3):
        ocopy(n, targets[n]).wait_send()

    @pl.loop(0, n_t)
    def _(t):
        pcopy(t).wait_send()
        xcopy(t).wait_send()

        @pl.when(t < n_c)
        def _():
            xin(t).wait_send()
            rel_y(t).wait_send()
            rel_p(t).wait_send()
            fwd_p(t).wait_send()
            ycopy(t).wait_send()

            @pl.when(t != c)
            def _():
                zcopy(t).wait_send()

    for n in range(4):
        rcopy(TS.at[n], tg_out.at[rblk(j), :], f_send.at[n], f_recv.at[n], d_y).wait_recv()
    for s in range(1, n_c):
        cz = lax.rem(c + s, n_c)
        rcopy(RO, rg_out.at[pl.ds(pl.multiple_of(cz * ch, ch), ch), :],
              w_send.at[s - 1], w_recv.at[cz], dev(i, cz, e)).wait_recv()
    own_o.wait()
    own_r.wait()


def fused(regions, table, shift, scale, labels, valid):
    n_i, n_c, n_e = (lax.axis_size(a) for a in ("img", "cls", "emb"))
    rows, width = regions.shape
    class_dev = table.shape[0]
    n_j = n_i * n_e
    blk = class_dev // n_j
    pad = -(-blk // 256) * 256
    ch = rows // n_c
    n_t = 2 * n_c
    imgs = valid.shape[0]
    full = n_e * width
    lanes = (rows // 128, 128)
    v = valid.astype(F32).reshape(imgs, n_j, blk).transpose(1, 0, 2)
    v = jnp.pad(v, ((0, 0), (0, 0), (0, pad - blk)))
    v = jnp.broadcast_to(v[:, :, None, :], (n_j, imgs, 8, pad))
    cfg = (n_i, n_c, n_e, rows, width, blk, pad, class_dev * n_c, imgs)
    dma = pltpu.SemaphoreType.DMA
    any_spec = pl.BlockSpec(memory_space=pl.ANY)
    loss, rg, tg = pl.pallas_call(
        functools.partial(kernel, cfg),
        out_shape=(
            jax.ShapeDtypeStruct((8, 128), F32),
            jax.ShapeDtypeStruct((rows, width), BF16),
            jax.ShapeDtypeStruct((class_dev, width), BF16),
        ),
        in_specs=[any_spec] * 6,
        out_specs=(pl.BlockSpec(memory_space=pltpu.VMEM), any_spec, any_spec),
        scratch_shapes=[
            pltpu.VMEM((n_i, rows, full), BF16),
            pltpu.VMEM((n_i * rows, full), BF16),
            pltpu.VMEM((pad, full), BF16),
            pltpu.VMEM((pad, n_i * rows), BF16),
            pltpu.VMEM((n_i,) + lanes, F32),
            pltpu.VMEM((n_i,) + lanes, F32),
            pltpu.VMEM((n_i,) + lanes, jnp.int32),
            pltpu.VMEM((n_i, imgs, 8, pad), F32),
            pltpu.VMEM((n_t, 2, ch, width), BF16),
            pltpu.VMEM((n_t, 2, ch, width), F32),
            pltpu.VMEM((n_t, 2, ch, width), BF16),
            pltpu.VMEM((n_t, ch, width), BF16),
            pltpu.VMEM((n_t, ch, width), BF16),
            pltpu.VMEM((n_c, ch, width), BF16),
            pltpu.VMEM((n_c, ch, width), BF16),
            pltpu.VMEM((n_c, ch, width), BF16),
            pltpu.VMEM((n_c, ch, width), BF16),
            pltpu.VMEM((ch, width), F32),
            pltpu.VMEM((4, blk, width), BF16),
            pltpu.VMEM((8, pad), F32),
            pltpu.VMEM((n_e, 8, 128), F32),
            pltpu.VMEM((n_i, 8, 128), F32),
            pltpu.VMEM((n_c, 8, 128), F32),
            pltpu.VMEM((n_e, 8, ch), F32),
            pltpu.VMEM((ch, width), BF16),
            dma((8,)), dma((3,)), dma((3,)), dma((4, n_c)), dma((4, n_c)),
            dma((3,)), dma((3,)), dma((4,)), dma((4,)),
            dma((n_t,)), dma((n_t,)), dma((n_t,)), dma((n_t,)),
            dma((n_c,)), dma((n_c,)), dma((n_c,)), dma((n_c,)),
            dma((4,)), dma((4,)), dma((4,)), dma((4,)),
            dma((n_c + 3,)), dma((1 + n_c + n_e,)), dma((3,)), dma((n_e,)),
            dma((n_c,)), dma((n_c,)),
        ],
        compiler_params=pltpu.CompilerParams(
            collective_id=0, has_side_effects=True, vmem_limit_bytes=60000 * 1024),
    )(regions, table, shift.reshape(lanes), scale.reshape(lanes), labels.reshape(lanes), v)
    return loss[0, 0], rg, tg


def focal(logit, target):
    prob = jax.nn.sigmoid(logit)
    return -0.25 * target * (1.0 - prob) ** 2 * jax.nn.log_sigmoid(logit) - 0.75 * (
        1.0 - target
    ) * prob**2 * jax.nn.log_sigmoid(-logit)


def generic(regions, table, shift, scale, labels, valid):
    rows = regions.shape[0]
    class_dev = table.shape[0]
    parts = lax.axis_size("emb")
    quarter = rows // parts
    start = lax.axis_index("emb") * quarter
    block = regions.astype(jnp.float32)
    squares = lax.psum(jnp.sum(block * block, axis=1), "emb")
    local_count = jnp.sum((labels >= 0).astype(jnp.float32))
    count = lax.psum(local_count, "img")
    inv = lax.rsqrt(squares + 1e-06)
    unit = block * inv[:, None]
    unit_b = unit.astype(jnp.bfloat16)
    unit_rows = lax.all_to_all(unit_b, "emb", split_axis=0, concat_axis=1, tiled=True)
    cosine = lax.dot_general(
        unit_rows,
        lax.all_gather(table, "emb", axis=1, tiled=True),
        (((1,), (1,)), ((), ())),
        preferred_element_type=jnp.float32,
    )
    shift_q = lax.dynamic_slice_in_dim(shift, start, quarter, 0)
    scale_q = lax.dynamic_slice_in_dim(scale, start, quarter, 0)
    label_q = lax.dynamic_slice_in_dim(labels, start, quarter, 0)
    image_ids = (start + jnp.arange(quarter, dtype=jnp.int32)) // (rows // valid.shape[0])
    onehot = (image_ids[:, None] == jnp.arange(valid.shape[0], dtype=jnp.int32)[None, :]).astype(
        jnp.float32
    )
    mask = jnp.dot(onehot, valid.astype(jnp.float32), preferred_element_type=jnp.float32)
    class_ids = lax.axis_index("cls") * class_dev + jnp.arange(class_dev, dtype=jnp.int32)
    logit = (cosine + shift_q[:, None]) * scale_q[:, None]
    target = (label_q[:, None] == class_ids[None, :]).astype(jnp.float32)
    term, pullback = jax.vjp(lambda value: focal(value, target), logit)
    dlogit = pullback(jnp.ones_like(term))[0]
    total = lax.psum(jnp.sum(term * mask), ("img", "cls", "emb"))
    factor = rows * lax.axis_size("img") / count
    dscore = (dlogit * mask * scale_q[:, None] * factor).astype(jnp.bfloat16)
    piece = lax.all_gather(dscore, "emb", axis=0, tiled=True)
    dunit_piece = jnp.dot(piece, table, preferred_element_type=jnp.float32)
    table_acc = lax.dot_general(
        piece, unit_b, (((0,), (0,)), ((), ())), preferred_element_type=jnp.float32
    )
    dunit = lax.psum(dunit_piece, "cls")
    radial = lax.psum(jnp.sum(unit * dunit, axis=1), "emb")
    region_grad = (inv[:, None] * (dunit - unit * radial[:, None])).astype(jnp.bfloat16)
    table_grad = lax.psum(table_acc, "img").astype(jnp.bfloat16)
    loss = total / count / (class_dev * lax.axis_size("cls"))
    return (loss, region_grad, table_grad)


def shards(*args):
    n_i, n_c, n_e = (lax.axis_size(a) for a in ("img", "cls", "emb"))
    rows, width = args[0].shape
    class_dev = args[1].shape[0]
    per_img = rows // args[5].shape[0]
    fits = n_i == 2 and n_c >= 3 and n_e == 4 and class_dev % (16 * n_i * n_e) == 0
    fits = fits and rows % (128 * n_c) == 0 and per_img % (rows // n_c) == 0
    fits = fits and width == 256
    return fused(*args) if fits else generic(*args)


def solution(mesh):
    placed = (P("img", "emb"), P("cls", "emb"), P("img"), P("img"), P("img"), P("img", "cls"))
    return jax.shard_map(
        shards,
        mesh=mesh,
        in_specs=placed,
        out_specs=(P(), P("img", "emb"), P("cls", "emb")),
        check_vma=False,
    )
```

```python
import functools

import jax
import jax.numpy as jnp
from jax import lax
from jax.experimental import pallas as pl
from jax.experimental.pallas import tpu as pltpu
from jax.sharding import PartitionSpec as P

MESH = pl.DeviceIdType.MESH
F32 = jnp.float32
BF16 = jnp.bfloat16


def kernel(cfg, regions, table, shift_in, scale_in, labels_in, valid, loss_out, rg_out, tg_out,
           RG, UN, TB, DS, SH, SL, LB, VB, SP, KP, PR, XS, XR, YS, YR, ZS, ZR, ZO,
           TS, LA, LE, LI, LC, RD, RO,
           loc, g_send, g_recv, gx_send, gx_recv, t_send, t_recv, s_send, s_recv,
           p_send, p_recv, x_send, x_recv, y_send, y_recv, z_send, z_recv,
           o_send, o_recv, f_send, f_recv, l_send, l_recv, r_send, r_recv,
           w_send, w_recv):
    n_i, n_c, n_e, rows, width, blk, pad, classes, imgs = cfg
    i, c, e = lax.axis_index("img"), lax.axis_index("cls"), lax.axis_index("emb")
    k = lax.rem(e, 2)
    x = e // 2
    oi = 1 - i
    part = 2 * x + 1 - k
    xn = 2 * (1 - x) + k
    xp = 2 * (1 - x) + 1 - k
    j = i * n_e + e
    ch = rows // n_c
    n_t = 2 * n_c
    full = n_e * width

    def dev(ii, cc, ee):
        return (ii, cc, ee)

    def rcopy(src, dst, ss, rs, d):
        return pltpu.make_async_remote_copy(
            src_ref=src, dst_ref=dst, send_sem=ss, recv_sem=rs,
            device_id=d, device_id_type=MESH)

    def cols(q):
        return pl.ds(pl.multiple_of(q * width, width), width)

    def rblk(q):
        return pl.ds(pl.multiple_of(q * blk, 16), blk)

    barrier = pltpu.get_barrier_semaphore()
    for ee in (part, xn, xp):
        pl.semaphore_signal(barrier, inc=1, device_id=dev(i, c, ee), device_id_type=MESH)
    pl.semaphore_signal(barrier, inc=1, device_id=dev(oi, c, e), device_id_type=MESH)
    for s in range(1, n_c):
        pl.semaphore_signal(barrier, inc=1, device_id=dev(i, lax.rem(c + s, n_c), e), device_id_type=MESH)
    pl.semaphore_wait(barrier, 3 + 1 + n_c - 1)

    d_part, d_xn, d_xp, d_y = dev(i, c, part), dev(i, c, xn), dev(i, c, xp), dev(oi, c, e)

    def rslice(im, m, q):
        return RG.at[im, pl.ds(pl.multiple_of(m * ch, ch), ch), cols(q)]

    def xin(m):
        return rcopy(regions.at[pl.ds(pl.multiple_of(m * ch, ch), ch), :], rslice(i, m, e),
                     gx_send.at[0, m], gx_recv.at[0, m], d_xn)

    def xin_wait(m):
        rcopy(rslice(i, m, xn), rslice(i, m, xn), gx_send.at[0, m], gx_recv.at[0, m], d_xn).wait_recv()

    def rel_y(m):
        return rcopy(rslice(i, m, xn), rslice(i, m, xn), gx_send.at[1, m], gx_recv.at[1, m], d_y)

    def rel_p(m):
        return rcopy(rslice(i, m, xn), rslice(i, m, xn), gx_send.at[2, m], gx_recv.at[2, m], d_part)

    def fwd_p(m):
        return rcopy(rslice(oi, m, xn), rslice(oi, m, xn), gx_send.at[3, m], gx_recv.at[3, m], d_part)

    def serve_x(m):
        xin_wait(m)
        rel_y(m).start()
        rel_p(m).start()

    def serve_y(m):
        rel_y(m).wait_recv()
        fwd_p(m).start()

    tcopies = []
    for n, ee in enumerate((xn, xp, part)):
        t = rcopy(table.at[rblk(i * n_e + ee), :], TB.at[pl.ds(0, blk), cols(e)],
                  t_send.at[n], t_recv.at[n], dev(i, c, ee))
        t.start()
        tcopies.append(t)
    smalls = []
    for n, (src, dst) in enumerate(((shift_in, SH), (scale_in, SL), (labels_in, LB),
                                    (valid.at[oi * n_e + e], VB))):
        q = rcopy(src, dst.at[i], s_send.at[n], s_recv.at[n], d_y)
        q.start()
        smalls.append(q)
    own_y = rcopy(regions, RG.at[i, :, cols(e)], g_send.at[0], g_recv.at[0], d_y)
    own_p = rcopy(regions, RG.at[i, :, cols(e)], g_send.at[1], g_recv.at[1], d_part)
    own_y.start()
    own_p.start()
    for m in range(n_c):
        xin(m).start()
    locs = [
        pltpu.make_async_copy(regions, RG.at[i, :, cols(e)], loc.at[0]),
        pltpu.make_async_copy(table.at[rblk(j), :], TB.at[pl.ds(0, blk), cols(e)], loc.at[1]),
        pltpu.make_async_copy(shift_in, SH.at[i], loc.at[2]),
        pltpu.make_async_copy(scale_in, SL.at[i], loc.at[3]),
        pltpu.make_async_copy(labels_in, LB.at[i], loc.at[6]),
        pltpu.make_async_copy(valid.at[j], VB.at[i], loc.at[7]),
    ]
    for q in locs:
        q.start()
    if pad > blk:
        TB[pl.ds(blk, pad - blk), :] = jnp.zeros((pad - blk, full), BF16)
    LA[...] = jnp.zeros_like(LA)

    own_y.wait_recv()
    fy1 = rcopy(RG.at[oi, :, cols(e)], RG.at[oi, :, cols(e)], g_send.at[2], g_recv.at[2], d_part)
    fy1.start()
    for q in locs:
        q.wait()
    for q in smalls:
        q.wait_recv()
    own_p.wait_recv()
    for t in tcopies:
        t.wait_recv()
    fy1.wait_recv()
    serve_x(0)

    fg = (LB[0] >= 0).astype(F32)
    for b in range(1, n_i):
        fg = fg + (LB[b] >= 0).astype(F32)
    count = jnp.sum(jnp.sum(fg, axis=0, keepdims=True), axis=1, keepdims=True)
    factor = (rows * n_i) / count

    base = (c * (n_i * n_e) + j) * blk
    class_ids = base + lax.broadcasted_iota(jnp.int32, (1, pad), 1)
    per_img = rows // imgs

    def column(ref, im, m):
        parts = []
        for b in range(ch // 128):
            row = ref[im, pl.ds(m * (ch // 128) + b, 1), :]
            parts.append(jnp.broadcast_to(row, (8, 128)).T[:, 0:1])
        return jnp.concatenate(parts, axis=0)

    def pcopy(t):
        return rcopy(SP.at[t], PR.at[t], p_send.at[t], p_recv.at[t], d_part)

    def xcopy(t):
        return rcopy(XS.at[t], XR.at[t], x_send.at[t], x_recv.at[t], d_xn)

    def ycopy(t):
        return rcopy(YS.at[t], YR.at[t], y_send.at[t], y_recv.at[t], d_y)

    def zcopy(m):
        return rcopy(ZS.at[m], ZR.at[c], z_send.at[m], z_recv.at[c], dev(i, m, e))

    def compute(im, m, t):
        r0 = pl.multiple_of(m * ch, ch)
        block = RG[im, pl.ds(r0, ch), :].astype(F32)
        inv = lax.rsqrt(jnp.sum(block * block, axis=1, keepdims=True) + 1e-06)
        unit_b = (block * inv).astype(BF16)
        u0 = pl.multiple_of(im * rows + m * ch, ch)
        UN[pl.ds(u0, ch), :] = unit_b
        cosine = lax.dot_general(unit_b, TB[...], (((1,), (1,)), ((), ())),
                                 preferred_element_type=F32)
        shift, scale, label = column(SH, im, m), column(SL, im, m), column(LB, im, m)
        mask = VB[im, (m * ch) // per_img][0:1, :]
        z = (cosine + shift) * scale
        hit = label == class_ids
        s = jnp.where(hit, -z, z)
        ex = jnp.exp(-jnp.abs(s))
        den = 1.0 + ex
        r = 1.0 / den
        er = ex * r
        pos = s >= 0
        q = jnp.where(pos, r, er)
        nq = jnp.where(pos, er, r)
        lg = jnp.where(ex < 0.01, ex * (1.0 - ex * (0.5 - ex * (1.0 / 3.0))), jnp.log(den))
        soft = jnp.maximum(s, 0.0) + lg
        wq = jnp.where(hit, 0.25, 0.75) * (q * q) * mask
        term = wq * soft
        LA[...] += jnp.sum(term.reshape(ch // 8, 8, pad), axis=0)
        g = wq * (q + 2.0 * nq * soft)
        g = jnp.where(hit, -g, g) * (scale * factor)
        ds = g.astype(BF16)
        DS[:, pl.ds(u0, ch)] = ds.T
        for xi in range(2):
            SP[t, xi] = jnp.dot(ds, TB[:, cols(2 * xi + 1 - k)], preferred_element_type=F32).astype(BF16)
            KP[t, xi] = jnp.dot(ds, TB[:, cols(2 * xi + k)], preferred_element_type=F32)

    def stage2(t):
        pcopy(t).wait_recv()
        XS[t] = (KP[t, 1 - x] + PR[t, 1 - x].astype(F32)).astype(BF16)
        xcopy(t).start()
        KP[t, x] = KP[t, x] + PR[t, x].astype(F32)

    def ocopy(n, q):
        return rcopy(TS.at[n], tg_out.at[rblk(j), :], o_send.at[n], o_recv.at[n], dev(i, c, q))

    targets = (xn, xp, part, e)
    def tg_of(n, q):
        TS[n] = jnp.dot(DS[0:blk, :], UN[:, cols(q)], preferred_element_type=F32).astype(BF16)

    def fcopy(n, q):
        src = TS.at[3] if n == 3 else tg_out.at[rblk(i * n_e + q), :]
        return rcopy(src, tg_out.at[rblk(i * n_e + q), :], f_send.at[n], f_recv.at[n], d_y)

    def slot_own(m):
        return jnp.where(m < 2, m, 2 * m - 2)

    def slot_other(m):
        return jnp.where(m < n_c - 2, 2 * m + 3, m + n_c)

    def stage3_other(m):
        t = slot_other(m)
        xcopy(t).wait_recv()
        YS[m] = (KP[t, x] + XR[t].astype(F32)).astype(BF16)
        ycopy(m).start()

    def stage3_own(m):
        t = slot_own(m)
        xcopy(t).wait_recv()
        val = KP[t, x] + XR[t].astype(F32)
        ycopy(m).wait_recv()
        tot = val + YR[m].astype(F32)

        @pl.when(m == c)
        def _():
            ZO[...] = tot

        @pl.when(m != c)
        def _():
            ZS[m] = tot.astype(BF16)
            zcopy(m).start()

    @pl.loop(0, n_t)
    def _(t):
        late = t >= 2 * (n_c - 1)
        odd = lax.rem(t, 2) == 1
        is_other = late | (odd & (t >= 2))
        m = jnp.where(t < 2, t, jnp.where(late, t - n_c, jnp.where(odd, (t - 3) // 2, t // 2 + 1)))
        im = jnp.where(is_other, oi, i)

        @pl.when(is_other)
        def _():
            fwd_p(m).wait_recv()

        @pl.when(jnp.logical_not(is_other))
        def _():
            rel_p(m).wait_recv()

        compute(im, m, t)

        @pl.when((t >= 1) & (t <= n_c))
        def _():
            serve_y(t - 1)

        @pl.when(t + 1 < n_c)
        def _():
            serve_x(t + 1)

        pcopy(t).start()

        @pl.when(t >= 1)
        def _():
            stage2(t - 1)

        @pl.when(t == n_t - 2)
        def _():
            stage3_other(0)

    tile = LA[:, 0:128]
    for b in range(1, pad // 128):
        tile = tile + LA[:, b * 128:(b + 1) * 128]
    LI[i] = tile
    li = rcopy(LI.at[i], LI.at[i], l_send.at[0], l_recv.at[0], d_y)
    li.start()
    tg_of(3, e)
    own_f = fcopy(3, e)
    own_f.start()
    stage2(n_t - 1)

    @pl.loop(0, 3)
    def _(b):
        n = lax.rem(b + 2, 3)
        q = 2 * jnp.where(n < 2, 1 - x, x) + jnp.where(n == 0, k, 1 - k)
        tg_of(n, q)
        ocopy(n, q).start()

    own_o = pltpu.make_async_copy(TS.at[3], tg_out.at[rblk(j), :], loc.at[4])
    own_o.start()

    for m in range(1, n_c):
        stage3_other(m)
    ocopy(2, part).wait_recv()
    part_f = fcopy(2, part)
    part_f.start()
    li.wait_recv()
    acc = LI[0]
    for b in range(1, n_i):
        acc = acc + LI[b]
    LC[c] = acc
    lz = []
    for s in range(1, n_c):
        q = rcopy(LC.at[c], LC.at[c], l_send.at[s], l_recv.at[1 + c], dev(i, lax.rem(c + s, n_c), e))
        q.start()
        lz.append(q)
    for m in range(n_c):
        stage3_own(m)
    fcs = [own_f, part_f]
    for n in (0, 1):
        q = targets[n]
        ocopy(n, q).wait_recv()
        fc = fcopy(n, q)
        fc.start()
        fcs.append(fc)

    for s in range(1, n_c):
        cz = lax.rem(c + s, n_c)
        rcopy(LC.at[cz], LC.at[cz], l_send.at[1], l_recv.at[1 + cz], dev(i, cz, e)).wait_recv()
    acc = LC[0]
    for b in range(1, n_c):
        acc = acc + LC[b]
    LE[e] = acc
    lcs = []
    for n, ee in enumerate((part, xn, xp)):
        lc = rcopy(LE.at[e], LE.at[e], l_send.at[n_c + n], l_recv.at[1 + n_c + e], dev(i, c, ee))
        lc.start()
        lcs.append(lc)

    for s in range(1, n_c):
        cz = lax.rem(c + s, n_c)
        rcopy(ZS.at[cz], ZR.at[cz], z_send.at[cz], z_recv.at[cz], dev(i, cz, e)).wait_recv()
    dun = ZO[...]
    for s in range(1, n_c):
        dun = dun + ZR[lax.rem(c + s, n_c)].astype(F32)
    r0 = pl.multiple_of(c * ch, ch)
    block = RG[i, pl.ds(r0, ch), :].astype(F32)
    inv = lax.rsqrt(jnp.sum(block * block, axis=1, keepdims=True) + 1e-06)
    unit = RG[i, pl.ds(r0, ch), cols(e)].astype(F32) * inv
    prod = unit * dun
    fold = prod[:, 0:128]
    for b in range(1, width // 128):
        fold = fold + prod[:, b * 128:(b + 1) * 128]
    rad = jnp.sum(fold.T, axis=0, keepdims=True)
    RD[e] = jnp.broadcast_to(rad, (8, ch))
    rcs = []
    for n, ee in enumerate((part, xn, xp)):
        rc = rcopy(RD.at[e], RD.at[e], r_send.at[n], r_recv.at[e], dev(i, c, ee))
        rc.start()
        rcs.append(rc)
    for ee in (part, xn, xp):
        rcopy(RD.at[ee], RD.at[ee], r_send.at[0], r_recv.at[ee], d_part).wait_recv()
    rsum = RD[0]
    for b in range(1, n_e):
        rsum = rsum + RD[b]
    radial = rsum.T[:, 0:1]
    RO[...] = (inv * (dun - unit * radial)).astype(BF16)
    wcs = []
    for s in range(1, n_c):
        q = rcopy(RO, rg_out.at[pl.ds(r0, ch), :], w_send.at[s - 1], w_recv.at[c], dev(i, lax.rem(c + s, n_c), e))
        q.start()
        wcs.append(q)
    own_r = pltpu.make_async_copy(RO, rg_out.at[pl.ds(r0, ch), :], loc.at[5])
    own_r.start()

    for ee in (part, xn, xp):
        rcopy(LE.at[ee], LE.at[ee], l_send.at[n_c], l_recv.at[1 + n_c + ee], d_part).wait_recv()
    acc = LE[0]
    for b in range(1, n_e):
        acc = acc + LE[b]
    total = jnp.sum(jnp.sum(acc, axis=0, keepdims=True), axis=1, keepdims=True)
    loss_out[...] = jnp.broadcast_to(total / count / classes, (8, 128))

    for q in [own_y, own_p, fy1] + smalls + tcopies + lcs + [li] + lz + rcs + wcs + fcs:
        q.wait_send()
    for n in range(3):
        ocopy(n, targets[n]).wait_send()

    @pl.loop(0, n_t)
    def _(t):
        pcopy(t).wait_send()
        xcopy(t).wait_send()

        @pl.when(t < n_c)
        def _():
            xin(t).wait_send()
            rel_y(t).wait_send()
            rel_p(t).wait_send()
            fwd_p(t).wait_send()
            ycopy(t).wait_send()

            @pl.when(t != c)
            def _():
                zcopy(t).wait_send()

    for n in range(4):
        rcopy(TS.at[n], tg_out.at[rblk(j), :], f_send.at[n], f_recv.at[n], d_y).wait_recv()
    for s in range(1, n_c):
        cz = lax.rem(c + s, n_c)
        rcopy(RO, rg_out.at[pl.ds(pl.multiple_of(cz * ch, ch), ch), :],
              w_send.at[s - 1], w_recv.at[cz], dev(i, cz, e)).wait_recv()
    own_o.wait()
    own_r.wait()


def settle(n_p, loss_in, rg_in, tg_in, loss_out, rg_out, tg_out, rg_v, tg_v, get, put):
    step = tg_in.shape[0] // n_p
    pieces = [(tg_in.at[pl.ds(b * step, step), :], tg_v.at[pl.ds(b * step, step), :],
               tg_out.at[pl.ds(b * step, step), :]) for b in range(n_p)]
    pieces.append((rg_in, rg_v, rg_out))
    ins = [pltpu.make_async_copy(a, v, get.at[n]) for n, (a, v, o) in enumerate(pieces)]
    outs = [pltpu.make_async_copy(v, o, put.at[n]) for n, (a, v, o) in enumerate(pieces)]
    for q in ins:
        q.start()
    loss_out[0, 0] = loss_in[0, 0]
    for a, o in zip(ins, outs):
        a.wait()
        o.start()
    for o in outs:
        o.wait()


def fused(regions, table, shift, scale, labels, valid):
    n_i, n_c, n_e = (lax.axis_size(a) for a in ("img", "cls", "emb"))
    rows, width = regions.shape
    class_dev = table.shape[0]
    n_j = n_i * n_e
    blk = class_dev // n_j
    pad = -(-blk // 256) * 256
    ch = rows // n_c
    n_t = 2 * n_c
    imgs = valid.shape[0]
    full = n_e * width
    lanes = (rows // 128, 128)
    v = valid.astype(F32).reshape(imgs, n_j, blk).transpose(1, 0, 2)
    v = jnp.pad(v, ((0, 0), (0, 0), (0, pad - blk)))
    v = jnp.broadcast_to(v[:, :, None, :], (n_j, imgs, 8, pad))
    cfg = (n_i, n_c, n_e, rows, width, blk, pad, class_dev * n_c, imgs)
    dma = pltpu.SemaphoreType.DMA
    any_spec = pl.BlockSpec(memory_space=pl.ANY)
    loss, rg, tg = pl.pallas_call(
        functools.partial(kernel, cfg),
        out_shape=(
            jax.ShapeDtypeStruct((8, 128), F32),
            jax.ShapeDtypeStruct((rows, width), BF16),
            jax.ShapeDtypeStruct((class_dev, width), BF16),
        ),
        in_specs=[any_spec] * 6,
        out_specs=(pl.BlockSpec(memory_space=pltpu.VMEM), any_spec, any_spec),
        scratch_shapes=[
            pltpu.VMEM((n_i, rows, full), BF16),
            pltpu.VMEM((n_i * rows, full), BF16),
            pltpu.VMEM((pad, full), BF16),
            pltpu.VMEM((pad, n_i * rows), BF16),
            pltpu.VMEM((n_i,) + lanes, F32),
            pltpu.VMEM((n_i,) + lanes, F32),
            pltpu.VMEM((n_i,) + lanes, jnp.int32),
            pltpu.VMEM((n_i, imgs, 8, pad), F32),
            pltpu.VMEM((n_t, 2, ch, width), BF16),
            pltpu.VMEM((n_t, 2, ch, width), F32),
            pltpu.VMEM((n_t, 2, ch, width), BF16),
            pltpu.VMEM((n_t, ch, width), BF16),
            pltpu.VMEM((n_t, ch, width), BF16),
            pltpu.VMEM((n_c, ch, width), BF16),
            pltpu.VMEM((n_c, ch, width), BF16),
            pltpu.VMEM((n_c, ch, width), BF16),
            pltpu.VMEM((n_c, ch, width), BF16),
            pltpu.VMEM((ch, width), F32),
            pltpu.VMEM((4, blk, width), BF16),
            pltpu.VMEM((8, pad), F32),
            pltpu.VMEM((n_e, 8, 128), F32),
            pltpu.VMEM((n_i, 8, 128), F32),
            pltpu.VMEM((n_c, 8, 128), F32),
            pltpu.VMEM((n_e, 8, ch), F32),
            pltpu.VMEM((ch, width), BF16),
            dma((8,)), dma((3,)), dma((3,)), dma((4, n_c)), dma((4, n_c)),
            dma((3,)), dma((3,)), dma((4,)), dma((4,)),
            dma((n_t,)), dma((n_t,)), dma((n_t,)), dma((n_t,)),
            dma((n_c,)), dma((n_c,)), dma((n_c,)), dma((n_c,)),
            dma((4,)), dma((4,)), dma((4,)), dma((4,)),
            dma((n_c + 3,)), dma((1 + n_c + n_e,)), dma((3,)), dma((n_e,)),
            dma((n_c,)), dma((n_c,)),
        ],
        compiler_params=pltpu.CompilerParams(
            collective_id=0, has_side_effects=True, vmem_limit_bytes=60000 * 1024),
    )(regions, table, shift.reshape(lanes), scale.reshape(lanes), labels.reshape(lanes), v)
    loss, rg, tg = pl.pallas_call(
        functools.partial(settle, n_j),
        out_shape=(
            jax.ShapeDtypeStruct((1, 1), F32),
            jax.ShapeDtypeStruct((rows, width), BF16),
            jax.ShapeDtypeStruct((class_dev, width), BF16),
        ),
        in_specs=[pl.BlockSpec(memory_space=pltpu.VMEM), any_spec, any_spec],
        out_specs=(pl.BlockSpec(memory_space=pltpu.SMEM), any_spec, any_spec),
        scratch_shapes=[
            pltpu.VMEM((rows, width), BF16),
            pltpu.VMEM((class_dev, width), BF16),
            dma((n_j + 1,)), dma((n_j + 1,)),
        ],
    )(loss, rg, tg)
    return loss[0, 0], rg, tg


def focal(logit, target):
    prob = jax.nn.sigmoid(logit)
    return -0.25 * target * (1.0 - prob) ** 2 * jax.nn.log_sigmoid(logit) - 0.75 * (
        1.0 - target
    ) * prob**2 * jax.nn.log_sigmoid(-logit)


def generic(regions, table, shift, scale, labels, valid):
    rows = regions.shape[0]
    class_dev = table.shape[0]
    parts = lax.axis_size("emb")
    quarter = rows // parts
    start = lax.axis_index("emb") * quarter
    block = regions.astype(jnp.float32)
    squares = lax.psum(jnp.sum(block * block, axis=1), "emb")
    local_count = jnp.sum((labels >= 0).astype(jnp.float32))
    count = lax.psum(local_count, "img")
    inv = lax.rsqrt(squares + 1e-06)
    unit = block * inv[:, None]
    unit_b = unit.astype(jnp.bfloat16)
    unit_rows = lax.all_to_all(unit_b, "emb", split_axis=0, concat_axis=1, tiled=True)
    cosine = lax.dot_general(
        unit_rows,
        lax.all_gather(table, "emb", axis=1, tiled=True),
        (((1,), (1,)), ((), ())),
        preferred_element_type=jnp.float32,
    )
    shift_q = lax.dynamic_slice_in_dim(shift, start, quarter, 0)
    scale_q = lax.dynamic_slice_in_dim(scale, start, quarter, 0)
    label_q = lax.dynamic_slice_in_dim(labels, start, quarter, 0)
    image_ids = (start + jnp.arange(quarter, dtype=jnp.int32)) // (rows // valid.shape[0])
    onehot = (image_ids[:, None] == jnp.arange(valid.shape[0], dtype=jnp.int32)[None, :]).astype(
        jnp.float32
    )
    mask = jnp.dot(onehot, valid.astype(jnp.float32), preferred_element_type=jnp.float32)
    class_ids = lax.axis_index("cls") * class_dev + jnp.arange(class_dev, dtype=jnp.int32)
    logit = (cosine + shift_q[:, None]) * scale_q[:, None]
    target = (label_q[:, None] == class_ids[None, :]).astype(jnp.float32)
    term, pullback = jax.vjp(lambda value: focal(value, target), logit)
    dlogit = pullback(jnp.ones_like(term))[0]
    total = lax.psum(jnp.sum(term * mask), ("img", "cls", "emb"))
    factor = rows * lax.axis_size("img") / count
    dscore = (dlogit * mask * scale_q[:, None] * factor).astype(jnp.bfloat16)
    piece = lax.all_gather(dscore, "emb", axis=0, tiled=True)
    dunit_piece = jnp.dot(piece, table, preferred_element_type=jnp.float32)
    table_acc = lax.dot_general(
        piece, unit_b, (((0,), (0,)), ((), ())), preferred_element_type=jnp.float32
    )
    dunit = lax.psum(dunit_piece, "cls")
    radial = lax.psum(jnp.sum(unit * dunit, axis=1), "emb")
    region_grad = (inv[:, None] * (dunit - unit * radial[:, None])).astype(jnp.bfloat16)
    table_grad = lax.psum(table_acc, "img").astype(jnp.bfloat16)
    loss = total / count / (class_dev * lax.axis_size("cls"))
    return (loss, region_grad, table_grad)


def shards(*args):
    n_i, n_c, n_e = (lax.axis_size(a) for a in ("img", "cls", "emb"))
    rows, width = args[0].shape
    class_dev = args[1].shape[0]
    per_img = rows // args[5].shape[0]
    fits = n_i == 2 and n_c >= 3 and n_e == 4 and class_dev % (16 * n_i * n_e) == 0
    fits = fits and rows % (128 * n_c) == 0 and per_img % (rows // n_c) == 0
    fits = fits and width == 256
    return fused(*args) if fits else generic(*args)


def solution(mesh):
    placed = (P("img", "emb"), P("cls", "emb"), P("img"), P("img"), P("img"), P("img", "cls"))
    return jax.shard_map(
        shards,
        mesh=mesh,
        in_specs=placed,
        out_specs=(P(), P("img", "emb"), P("cls", "emb")),
        check_vma=False,
    )
```

```python
import functools

import jax
import jax.numpy as jnp
from jax import lax
from jax.experimental import pallas as pl
from jax.experimental.pallas import tpu as pltpu
from jax.sharding import PartitionSpec as P

MESH = pl.DeviceIdType.MESH
F32 = jnp.float32
BF16 = jnp.bfloat16


def kernel(cfg, regions, table, shift_in, scale_in, labels_in, valid, loss_out, rg_out, tg_out,
           RG, UN, TB, DS, SH, SL, LB, VB, SP, KP, PR, XS, XR, YS, YR, ZS, ZR, ZO,
           TS, LA, LE, LI, LC, RD, RO,
           loc, g_send, g_recv, gx_send, gx_recv, t_send, t_recv, s_send, s_recv,
           p_send, p_recv, x_send, x_recv, y_send, y_recv, z_send, z_recv,
           o_send, o_recv, f_send, f_recv, l_send, l_recv, r_send, r_recv,
           w_send, w_recv):
    n_i, n_c, n_e, rows, width, blk, pad, classes, imgs = cfg
    i, c, e = lax.axis_index("img"), lax.axis_index("cls"), lax.axis_index("emb")
    k = lax.rem(e, 2)
    x = e // 2
    oi = 1 - i
    part = 2 * x + 1 - k
    xn = 2 * (1 - x) + k
    xp = 2 * (1 - x) + 1 - k
    j = i * n_e + e
    ch = rows // n_c
    n_t = 2 * n_c
    full = n_e * width

    def dev(ii, cc, ee):
        return (ii, cc, ee)

    def rcopy(src, dst, ss, rs, d):
        return pltpu.make_async_remote_copy(
            src_ref=src, dst_ref=dst, send_sem=ss, recv_sem=rs,
            device_id=d, device_id_type=MESH)

    def cols(q):
        return pl.ds(pl.multiple_of(q * width, width), width)

    def rblk(q):
        return pl.ds(pl.multiple_of(q * blk, 16), blk)

    barrier = pltpu.get_barrier_semaphore()
    for ee in (part, xn, xp):
        pl.semaphore_signal(barrier, inc=1, device_id=dev(i, c, ee), device_id_type=MESH)
    pl.semaphore_signal(barrier, inc=1, device_id=dev(oi, c, e), device_id_type=MESH)
    for s in range(1, n_c):
        pl.semaphore_signal(barrier, inc=1, device_id=dev(i, lax.rem(c + s, n_c), e), device_id_type=MESH)
    pl.semaphore_wait(barrier, 3 + 1 + n_c - 1)

    d_part, d_xn, d_xp, d_y = dev(i, c, part), dev(i, c, xn), dev(i, c, xp), dev(oi, c, e)

    def rslice(im, m, q):
        return RG.at[im, pl.ds(pl.multiple_of(m * ch, ch), ch), cols(q)]

    def xin(m):
        return rcopy(regions.at[pl.ds(pl.multiple_of(m * ch, ch), ch), :], rslice(i, m, e),
                     gx_send.at[0, m], gx_recv.at[0, m], d_xn)

    def xin_wait(m):
        rcopy(rslice(i, m, xn), rslice(i, m, xn), gx_send.at[0, m], gx_recv.at[0, m], d_xn).wait_recv()

    def rel_y(m):
        return rcopy(rslice(i, m, xn), rslice(i, m, xn), gx_send.at[1, m], gx_recv.at[1, m], d_y)

    def rel_p(m):
        return rcopy(rslice(i, m, xn), rslice(i, m, xn), gx_send.at[2, m], gx_recv.at[2, m], d_part)

    def fwd_p(m):
        return rcopy(rslice(oi, m, xn), rslice(oi, m, xn), gx_send.at[3, m], gx_recv.at[3, m], d_part)

    def serve_x(m):
        xin_wait(m)
        rel_y(m).start()
        rel_p(m).start()

    def serve_y(m):
        rel_y(m).wait_recv()
        fwd_p(m).start()

    tcopies = []
    for n, ee in enumerate((xn, xp, part)):
        t = rcopy(table.at[rblk(i * n_e + ee), :], TB.at[pl.ds(0, blk), cols(e)],
                  t_send.at[n], t_recv.at[n], dev(i, c, ee))
        t.start()
        tcopies.append(t)
    smalls = []
    for n, (src, dst) in enumerate(((shift_in, SH), (scale_in, SL), (labels_in, LB),
                                    (valid.at[oi * n_e + e], VB))):
        q = rcopy(src, dst.at[i], s_send.at[n], s_recv.at[n], d_y)
        q.start()
        smalls.append(q)
    own_y = rcopy(regions, RG.at[i, :, cols(e)], g_send.at[0], g_recv.at[0], d_y)
    own_p = rcopy(regions, RG.at[i, :, cols(e)], g_send.at[1], g_recv.at[1], d_part)
    own_y.start()
    own_p.start()
    for m in range(n_c):
        xin(m).start()
    locs = [
        pltpu.make_async_copy(regions, RG.at[i, :, cols(e)], loc.at[0]),
        pltpu.make_async_copy(table.at[rblk(j), :], TB.at[pl.ds(0, blk), cols(e)], loc.at[1]),
        pltpu.make_async_copy(shift_in, SH.at[i], loc.at[2]),
        pltpu.make_async_copy(scale_in, SL.at[i], loc.at[3]),
        pltpu.make_async_copy(labels_in, LB.at[i], loc.at[6]),
        pltpu.make_async_copy(valid.at[j], VB.at[i], loc.at[7]),
    ]
    for q in locs:
        q.start()
    if pad > blk:
        TB[pl.ds(blk, pad - blk), :] = jnp.zeros((pad - blk, full), BF16)
    LA[...] = jnp.zeros_like(LA)

    own_y.wait_recv()
    fy1 = rcopy(RG.at[oi, :, cols(e)], RG.at[oi, :, cols(e)], g_send.at[2], g_recv.at[2], d_part)
    fy1.start()
    for q in locs:
        q.wait()
    for q in smalls:
        q.wait_recv()
    own_p.wait_recv()
    for t in tcopies:
        t.wait_recv()
    fy1.wait_recv()
    serve_x(0)

    fg = (LB[0] >= 0).astype(F32)
    for b in range(1, n_i):
        fg = fg + (LB[b] >= 0).astype(F32)
    count = jnp.sum(jnp.sum(fg, axis=0, keepdims=True), axis=1, keepdims=True)
    factor = (rows * n_i) / count

    base = (c * (n_i * n_e) + j) * blk
    class_ids = base + lax.broadcasted_iota(jnp.int32, (1, pad), 1)
    per_img = rows // imgs

    def column(ref, im, m):
        parts = []
        for b in range(ch // 128):
            row = ref[im, pl.ds(m * (ch // 128) + b, 1), :]
            parts.append(jnp.broadcast_to(row, (8, 128)).T[:, 0:1])
        return jnp.concatenate(parts, axis=0)

    def pcopy(t):
        return rcopy(SP.at[t], PR.at[t], p_send.at[t], p_recv.at[t], d_part)

    def xcopy(t):
        return rcopy(XS.at[t], XR.at[t], x_send.at[t], x_recv.at[t], d_xn)

    def ycopy(t):
        return rcopy(YS.at[t], YR.at[t], y_send.at[t], y_recv.at[t], d_y)

    def zcopy(m):
        return rcopy(ZS.at[m], ZR.at[c], z_send.at[m], z_recv.at[c], dev(i, m, e))

    def compute(im, m, t):
        r0 = pl.multiple_of(m * ch, ch)
        block = RG[im, pl.ds(r0, ch), :].astype(F32)
        inv = lax.rsqrt(jnp.sum(block * block, axis=1, keepdims=True) + 1e-06)
        unit_b = (block * inv).astype(BF16)
        u0 = pl.multiple_of(im * rows + m * ch, ch)
        UN[pl.ds(u0, ch), :] = unit_b
        cosine = lax.dot_general(unit_b, TB[...], (((1,), (1,)), ((), ())),
                                 preferred_element_type=F32)
        shift, scale, label = column(SH, im, m), column(SL, im, m), column(LB, im, m)
        mask = VB[im, (m * ch) // per_img][0:1, :]
        z = (cosine + shift) * scale
        hit = label == class_ids
        s = jnp.where(hit, -z, z)
        ex = jnp.exp(-jnp.abs(s))
        den = 1.0 + ex
        r = 1.0 / den
        er = ex * r
        pos = s >= 0
        q = jnp.where(pos, r, er)
        nq = jnp.where(pos, er, r)
        lg = jnp.where(ex < 0.01, ex * (1.0 - ex * (0.5 - ex * (1.0 / 3.0))), jnp.log(den))
        soft = jnp.maximum(s, 0.0) + lg
        wq = jnp.where(hit, 0.25, 0.75) * (q * q) * mask
        term = wq * soft
        LA[...] += jnp.sum(term.reshape(ch // 8, 8, pad), axis=0)
        g = wq * (q + 2.0 * nq * soft)
        g = jnp.where(hit, -g, g) * (scale * factor)
        ds = g.astype(BF16)
        DS[:, pl.ds(u0, ch)] = ds.T
        for xi in range(2):
            SP[t, xi] = jnp.dot(ds, TB[:, cols(2 * xi + 1 - k)], preferred_element_type=F32).astype(BF16)
            KP[t, xi] = jnp.dot(ds, TB[:, cols(2 * xi + k)], preferred_element_type=F32)

    def stage2(t):
        pcopy(t).wait_recv()
        XS[t] = (KP[t, 1 - x] + PR[t, 1 - x].astype(F32)).astype(BF16)
        xcopy(t).start()
        KP[t, x] = KP[t, x] + PR[t, x].astype(F32)

    def ocopy(n, q):
        return rcopy(TS.at[n], tg_out.at[rblk(j), :], o_send.at[n], o_recv.at[n], dev(i, c, q))

    targets = (xn, xp, part, e)
    def tg_of(n, q):
        TS[n] = jnp.dot(DS[0:blk, :], UN[:, cols(q)], preferred_element_type=F32).astype(BF16)

    def fcopy(n, q):
        src = TS.at[3] if n == 3 else tg_out.at[rblk(i * n_e + q), :]
        return rcopy(src, tg_out.at[rblk(i * n_e + q), :], f_send.at[n], f_recv.at[n], d_y)

    def slot_own(m):
        return jnp.where(m < 2, m, jnp.where(m == n_c - 1, 2 * m - 1, 2 * m - 2))

    def slot_other(m):
        return jnp.where(m < n_c - 2, jnp.where(m == n_c - 3, 2 * m + 2, 2 * m + 3), m + n_c)

    def stage3_other(m):
        t = slot_other(m)
        xcopy(t).wait_recv()
        YS[m] = (KP[t, x] + XR[t].astype(F32)).astype(BF16)
        ycopy(m).start()

    def stage3_own(m):
        t = slot_own(m)
        xcopy(t).wait_recv()
        val = KP[t, x] + XR[t].astype(F32)
        ycopy(m).wait_recv()
        tot = val + YR[m].astype(F32)

        @pl.when(m == c)
        def _():
            ZO[...] = tot

        @pl.when(m != c)
        def _():
            ZS[m] = tot.astype(BF16)
            zcopy(m).start()

    @pl.loop(0, n_t)
    def _(t):
        late = t >= 2 * (n_c - 1)
        w = jnp.where(t == 2 * n_c - 4, t + 1, jnp.where(t == 2 * n_c - 3, t - 1, t))
        odd = lax.rem(w, 2) == 1
        is_other = late | (odd & (t >= 2))
        m = jnp.where(t < 2, t, jnp.where(late, t - n_c, jnp.where(odd, (w - 3) // 2, w // 2 + 1)))
        im = jnp.where(is_other, oi, i)

        @pl.when(is_other)
        def _():
            fwd_p(m).wait_recv()

        @pl.when(jnp.logical_not(is_other))
        def _():
            rel_p(m).wait_recv()

        compute(im, m, t)

        @pl.when((t >= 1) & (t <= n_c))
        def _():
            serve_y(t - 1)

        @pl.when(t + 1 < n_c)
        def _():
            serve_x(t + 1)

        pcopy(t).start()

        @pl.when(t >= 1)
        def _():
            stage2(t - 1)

        @pl.when(t == n_t - 2)
        def _():
            stage3_other(0)

    tile = LA[:, 0:128]
    for b in range(1, pad // 128):
        tile = tile + LA[:, b * 128:(b + 1) * 128]
    LI[i] = tile
    li = rcopy(LI.at[i], LI.at[i], l_send.at[0], l_recv.at[0], d_y)
    li.start()
    tg_of(3, e)
    own_f = fcopy(3, e)
    own_f.start()
    stage2(n_t - 1)

    @pl.loop(0, 3)
    def _(b):
        n = lax.rem(b + 2, 3)
        q = 2 * jnp.where(n < 2, 1 - x, x) + jnp.where(n == 0, k, 1 - k)
        tg_of(n, q)
        ocopy(n, q).start()

    own_o = pltpu.make_async_copy(TS.at[3], tg_out.at[rblk(j), :], loc.at[4])
    own_o.start()

    for m in range(1, n_c):
        stage3_other(m)
    ocopy(2, part).wait_recv()
    part_f = fcopy(2, part)
    part_f.start()
    li.wait_recv()
    acc = LI[0]
    for b in range(1, n_i):
        acc = acc + LI[b]
    LC[c] = acc
    lz = []
    for s in range(1, n_c):
        q = rcopy(LC.at[c], LC.at[c], l_send.at[s], l_recv.at[1 + c], dev(i, lax.rem(c + s, n_c), e))
        q.start()
        lz.append(q)
    for m in range(n_c):
        stage3_own(m)
    fcs = [own_f, part_f]
    for n in (0, 1):
        q = targets[n]
        ocopy(n, q).wait_recv()
        fc = fcopy(n, q)
        fc.start()
        fcs.append(fc)

    for s in range(1, n_c):
        cz = lax.rem(c + s, n_c)
        rcopy(LC.at[cz], LC.at[cz], l_send.at[1], l_recv.at[1 + cz], dev(i, cz, e)).wait_recv()
    acc = LC[0]
    for b in range(1, n_c):
        acc = acc + LC[b]
    LE[e] = acc
    lcs = []
    for n, ee in enumerate((part, xn, xp)):
        lc = rcopy(LE.at[e], LE.at[e], l_send.at[n_c + n], l_recv.at[1 + n_c + e], dev(i, c, ee))
        lc.start()
        lcs.append(lc)

    for s in range(1, n_c):
        cz = lax.rem(c + s, n_c)
        rcopy(ZS.at[cz], ZR.at[cz], z_send.at[cz], z_recv.at[cz], dev(i, cz, e)).wait_recv()
    dun = ZO[...]
    for s in range(1, n_c):
        dun = dun + ZR[lax.rem(c + s, n_c)].astype(F32)
    r0 = pl.multiple_of(c * ch, ch)
    block = RG[i, pl.ds(r0, ch), :].astype(F32)
    inv = lax.rsqrt(jnp.sum(block * block, axis=1, keepdims=True) + 1e-06)
    unit = RG[i, pl.ds(r0, ch), cols(e)].astype(F32) * inv
    prod = unit * dun
    fold = prod[:, 0:128]
    for b in range(1, width // 128):
        fold = fold + prod[:, b * 128:(b + 1) * 128]
    rad = jnp.sum(fold.T, axis=0, keepdims=True)
    RD[e] = jnp.broadcast_to(rad, (8, ch))
    rcs = []
    for n, ee in enumerate((part, xn, xp)):
        rc = rcopy(RD.at[e], RD.at[e], r_send.at[n], r_recv.at[e], dev(i, c, ee))
        rc.start()
        rcs.append(rc)
    for ee in (part, xn, xp):
        rcopy(RD.at[ee], RD.at[ee], r_send.at[0], r_recv.at[ee], d_part).wait_recv()
    rsum = RD[0]
    for b in range(1, n_e):
        rsum = rsum + RD[b]
    radial = rsum.T[:, 0:1]
    RO[...] = (inv * (dun - unit * radial)).astype(BF16)
    wcs = []
    for s in range(1, n_c):
        q = rcopy(RO, rg_out.at[pl.ds(r0, ch), :], w_send.at[s - 1], w_recv.at[c], dev(i, lax.rem(c + s, n_c), e))
        q.start()
        wcs.append(q)
    own_r = pltpu.make_async_copy(RO, rg_out.at[pl.ds(r0, ch), :], loc.at[5])
    own_r.start()

    for ee in (part, xn, xp):
        rcopy(LE.at[ee], LE.at[ee], l_send.at[n_c], l_recv.at[1 + n_c + ee], d_part).wait_recv()
    acc = LE[0]
    for b in range(1, n_e):
        acc = acc + LE[b]
    total = jnp.sum(jnp.sum(acc, axis=0, keepdims=True), axis=1, keepdims=True)
    loss_out[...] = jnp.broadcast_to(total / count / classes, (8, 128))

    for q in [own_y, own_p, fy1] + smalls + tcopies + lcs + [li] + lz + rcs + wcs + fcs:
        q.wait_send()
    for n in range(3):
        ocopy(n, targets[n]).wait_send()

    @pl.loop(0, n_t)
    def _(t):
        pcopy(t).wait_send()
        xcopy(t).wait_send()

        @pl.when(t < n_c)
        def _():
            xin(t).wait_send()
            rel_y(t).wait_send()
            rel_p(t).wait_send()
            fwd_p(t).wait_send()
            ycopy(t).wait_send()

            @pl.when(t != c)
            def _():
                zcopy(t).wait_send()

    for n in range(4):
        rcopy(TS.at[n], tg_out.at[rblk(j), :], f_send.at[n], f_recv.at[n], d_y).wait_recv()
    for s in range(1, n_c):
        cz = lax.rem(c + s, n_c)
        rcopy(RO, rg_out.at[pl.ds(pl.multiple_of(cz * ch, ch), ch), :],
              w_send.at[s - 1], w_recv.at[cz], dev(i, cz, e)).wait_recv()
    own_o.wait()
    own_r.wait()


def settle(n_p, loss_in, rg_in, tg_in, loss_out, rg_out, tg_out, rg_v, tg_v, get, put):
    step = tg_in.shape[0] // n_p
    pieces = [(tg_in.at[pl.ds(b * step, step), :], tg_v.at[pl.ds(b * step, step), :],
               tg_out.at[pl.ds(b * step, step), :]) for b in range(n_p)]
    pieces.append((rg_in, rg_v, rg_out))
    ins = [pltpu.make_async_copy(a, v, get.at[n]) for n, (a, v, o) in enumerate(pieces)]
    outs = [pltpu.make_async_copy(v, o, put.at[n]) for n, (a, v, o) in enumerate(pieces)]
    for q in ins:
        q.start()
    loss_out[0, 0] = loss_in[0, 0]
    for a, o in zip(ins, outs):
        a.wait()
        o.start()
    for o in outs:
        o.wait()


def fused(regions, table, shift, scale, labels, valid):
    n_i, n_c, n_e = (lax.axis_size(a) for a in ("img", "cls", "emb"))
    rows, width = regions.shape
    class_dev = table.shape[0]
    n_j = n_i * n_e
    blk = class_dev // n_j
    pad = -(-blk // 256) * 256
    ch = rows // n_c
    n_t = 2 * n_c
    imgs = valid.shape[0]
    full = n_e * width
    lanes = (rows // 128, 128)
    v = valid.astype(F32).reshape(imgs, n_j, blk).transpose(1, 0, 2)
    v = jnp.pad(v, ((0, 0), (0, 0), (0, pad - blk)))
    v = jnp.broadcast_to(v[:, :, None, :], (n_j, imgs, 8, pad))
    cfg = (n_i, n_c, n_e, rows, width, blk, pad, class_dev * n_c, imgs)
    dma = pltpu.SemaphoreType.DMA
    any_spec = pl.BlockSpec(memory_space=pl.ANY)
    loss, rg, tg = pl.pallas_call(
        functools.partial(kernel, cfg),
        out_shape=(
            jax.ShapeDtypeStruct((8, 128), F32),
            jax.ShapeDtypeStruct((rows, width), BF16),
            jax.ShapeDtypeStruct((class_dev, width), BF16),
        ),
        in_specs=[any_spec] * 6,
        out_specs=(pl.BlockSpec(memory_space=pltpu.VMEM), any_spec, any_spec),
        scratch_shapes=[
            pltpu.VMEM((n_i, rows, full), BF16),
            pltpu.VMEM((n_i * rows, full), BF16),
            pltpu.VMEM((pad, full), BF16),
            pltpu.VMEM((pad, n_i * rows), BF16),
            pltpu.VMEM((n_i,) + lanes, F32),
            pltpu.VMEM((n_i,) + lanes, F32),
            pltpu.VMEM((n_i,) + lanes, jnp.int32),
            pltpu.VMEM((n_i, imgs, 8, pad), F32),
            pltpu.VMEM((n_t, 2, ch, width), BF16),
            pltpu.VMEM((n_t, 2, ch, width), F32),
            pltpu.VMEM((n_t, 2, ch, width), BF16),
            pltpu.VMEM((n_t, ch, width), BF16),
            pltpu.VMEM((n_t, ch, width), BF16),
            pltpu.VMEM((n_c, ch, width), BF16),
            pltpu.VMEM((n_c, ch, width), BF16),
            pltpu.VMEM((n_c, ch, width), BF16),
            pltpu.VMEM((n_c, ch, width), BF16),
            pltpu.VMEM((ch, width), F32),
            pltpu.VMEM((4, blk, width), BF16),
            pltpu.VMEM((8, pad), F32),
            pltpu.VMEM((n_e, 8, 128), F32),
            pltpu.VMEM((n_i, 8, 128), F32),
            pltpu.VMEM((n_c, 8, 128), F32),
            pltpu.VMEM((n_e, 8, ch), F32),
            pltpu.VMEM((ch, width), BF16),
            dma((8,)), dma((3,)), dma((3,)), dma((4, n_c)), dma((4, n_c)),
            dma((3,)), dma((3,)), dma((4,)), dma((4,)),
            dma((n_t,)), dma((n_t,)), dma((n_t,)), dma((n_t,)),
            dma((n_c,)), dma((n_c,)), dma((n_c,)), dma((n_c,)),
            dma((4,)), dma((4,)), dma((4,)), dma((4,)),
            dma((n_c + 3,)), dma((1 + n_c + n_e,)), dma((3,)), dma((n_e,)),
            dma((n_c,)), dma((n_c,)),
        ],
        compiler_params=pltpu.CompilerParams(
            collective_id=0, has_side_effects=True, vmem_limit_bytes=60000 * 1024),
    )(regions, table, shift.reshape(lanes), scale.reshape(lanes), labels.reshape(lanes), v)
    loss, rg, tg = pl.pallas_call(
        functools.partial(settle, n_j),
        out_shape=(
            jax.ShapeDtypeStruct((1, 1), F32),
            jax.ShapeDtypeStruct((rows, width), BF16),
            jax.ShapeDtypeStruct((class_dev, width), BF16),
        ),
        in_specs=[pl.BlockSpec(memory_space=pltpu.VMEM), any_spec, any_spec],
        out_specs=(pl.BlockSpec(memory_space=pltpu.SMEM), any_spec, any_spec),
        scratch_shapes=[
            pltpu.VMEM((rows, width), BF16),
            pltpu.VMEM((class_dev, width), BF16),
            dma((n_j + 1,)), dma((n_j + 1,)),
        ],
    )(loss, rg, tg)
    return loss[0, 0], rg, tg


def focal(logit, target):
    prob = jax.nn.sigmoid(logit)
    return -0.25 * target * (1.0 - prob) ** 2 * jax.nn.log_sigmoid(logit) - 0.75 * (
        1.0 - target
    ) * prob**2 * jax.nn.log_sigmoid(-logit)


def generic(regions, table, shift, scale, labels, valid):
    rows = regions.shape[0]
    class_dev = table.shape[0]
    parts = lax.axis_size("emb")
    quarter = rows // parts
    start = lax.axis_index("emb") * quarter
    block = regions.astype(jnp.float32)
    squares = lax.psum(jnp.sum(block * block, axis=1), "emb")
    local_count = jnp.sum((labels >= 0).astype(jnp.float32))
    count = lax.psum(local_count, "img")
    inv = lax.rsqrt(squares + 1e-06)
    unit = block * inv[:, None]
    unit_b = unit.astype(jnp.bfloat16)
    unit_rows = lax.all_to_all(unit_b, "emb", split_axis=0, concat_axis=1, tiled=True)
    cosine = lax.dot_general(
        unit_rows,
        lax.all_gather(table, "emb", axis=1, tiled=True),
        (((1,), (1,)), ((), ())),
        preferred_element_type=jnp.float32,
    )
    shift_q = lax.dynamic_slice_in_dim(shift, start, quarter, 0)
    scale_q = lax.dynamic_slice_in_dim(scale, start, quarter, 0)
    label_q = lax.dynamic_slice_in_dim(labels, start, quarter, 0)
    image_ids = (start + jnp.arange(quarter, dtype=jnp.int32)) // (rows // valid.shape[0])
    onehot = (image_ids[:, None] == jnp.arange(valid.shape[0], dtype=jnp.int32)[None, :]).astype(
        jnp.float32
    )
    mask = jnp.dot(onehot, valid.astype(jnp.float32), preferred_element_type=jnp.float32)
    class_ids = lax.axis_index("cls") * class_dev + jnp.arange(class_dev, dtype=jnp.int32)
    logit = (cosine + shift_q[:, None]) * scale_q[:, None]
    target = (label_q[:, None] == class_ids[None, :]).astype(jnp.float32)
    term, pullback = jax.vjp(lambda value: focal(value, target), logit)
    dlogit = pullback(jnp.ones_like(term))[0]
    total = lax.psum(jnp.sum(term * mask), ("img", "cls", "emb"))
    factor = rows * lax.axis_size("img") / count
    dscore = (dlogit * mask * scale_q[:, None] * factor).astype(jnp.bfloat16)
    piece = lax.all_gather(dscore, "emb", axis=0, tiled=True)
    dunit_piece = jnp.dot(piece, table, preferred_element_type=jnp.float32)
    table_acc = lax.dot_general(
        piece, unit_b, (((0,), (0,)), ((), ())), preferred_element_type=jnp.float32
    )
    dunit = lax.psum(dunit_piece, "cls")
    radial = lax.psum(jnp.sum(unit * dunit, axis=1), "emb")
    region_grad = (inv[:, None] * (dunit - unit * radial[:, None])).astype(jnp.bfloat16)
    table_grad = lax.psum(table_acc, "img").astype(jnp.bfloat16)
    loss = total / count / (class_dev * lax.axis_size("cls"))
    return (loss, region_grad, table_grad)


def shards(*args):
    n_i, n_c, n_e = (lax.axis_size(a) for a in ("img", "cls", "emb"))
    rows, width = args[0].shape
    class_dev = args[1].shape[0]
    per_img = rows // args[5].shape[0]
    fits = n_i == 2 and n_c >= 3 and n_e == 4 and class_dev % (16 * n_i * n_e) == 0
    fits = fits and rows % (128 * n_c) == 0 and per_img % (rows // n_c) == 0
    fits = fits and width == 256
    return fused(*args) if fits else generic(*args)


def solution(mesh):
    placed = (P("img", "emb"), P("cls", "emb"), P("img"), P("img"), P("img"), P("img", "cls"))
    return jax.shard_map(
        shards,
        mesh=mesh,
        in_specs=placed,
        out_specs=(P(), P("img", "emb"), P("cls", "emb")),
        check_vma=False,
    )
```
